256 devices in a mesh: blk: 128 (over x_hi, y, z, core), head: 2 (over x_lo).
Axes of the slice: x: 4 (x_hi: 2, x_lo: 2; x = x_hi * 2 + x_lo), y: 4, z: 8, core: 2. Of those that a mesh axis runs over, the one named last changes fastest.
Arguments:
- query: bfloat16 [32768, 1024], P('blk', 'head'), may hold values from -192 to 192
- key: bfloat16 [32768, 1024], P('blk', 'head'), may hold values from -6 to 6
- value: bfloat16 [32768, 1024], P('blk', 'head'), may hold values from -6 to 6
- out_grad: bfloat16 [32768, 1024], P('blk', 'head'), may hold values from -48 to 48
- q_weight: bfloat16 [1024, 1024], P(None, 'head'), may hold values from -0.1875 to 0.1875
- k_weight: bfloat16 [1024, 1024], P(None, 'head'), may hold values from -0.1875 to 0.1875
- v_weight: bfloat16 [1024, 1024], P(None, 'head'), may hold values from -0.1875 to 0.1875
- adjacency: int32 [256, 14], P('blk'), may hold values from 0 to 1, as said below
- owner: int32 [32768, 1], P('blk'), may hold values from 0 to 127; in each aligned block of 256 rows (0 to 255, 256 to 511, ...) at most 4 rows name the same one
Outputs:
- grad_input: bfloat16 [65536, 1024], P('blk', 'head')
The draws below stay inside these ranges and needn't reach their ends.
Inputs may be any that keep to these rules, and one draw needn't show every extreme that they name: adjacency[b, c] is 1 where the hits of block b attend the hits of key block c mod 2 of the sector c // 2 - 3 places further along the cycle. Among the hits of one sector at most 4 have the same owner, and that many do in some sectors.
All inputs are finite; a program needn't handle non-finite values.
Results may differ from the reference program's by a relative error of at most 0.017.
Values may be sent and summed in bfloat16 or wider, within the bound.
No kernel may reach another device: no remote copies, remote signals or barrier semaphores. Data moves between devices by JAX's collectives and lax.ppermute only.
A program may use at most 64 MiB of HBM per device.

```python
import math
import jax
import jax.numpy as jnp
import numpy as np
from jax import lax

D = 1024
H = 16
HD = 64
HITS_DEV = 256
BLOCK = 128
REACH = 3
BLK_DEV = 2
SECTORS = 128
HITS = 32768
CAP = 4


def base_keys(key):
    return jnp.clip(jax.random.normal(jax.random.fold_in(key, 101), (HITS, H * HD), jnp.float32), -6.0, 6.0)


def draw_key(key, part):
    keys_all = base_keys(key)
    return keys_all.astype(jnp.bfloat16)


def draw_query(key, part):
    queries = jnp.clip(jax.random.normal(jax.random.fold_in(key, 202), (HITS, H * HD), jnp.float32), -6.0, 6.0)
    return queries.astype(jnp.bfloat16)


def draw_adjacency(key, part):
    level = jax.random.randint(jax.random.fold_in(key, 303), (SECTORS, 1, 1), 1, 9)
    pattern = jax.random.randint(jax.random.fold_in(key, 304), (SECTORS, BLK_DEV, (2 * REACH + 1) * BLK_DEV), 0, 8)
    return (pattern < level).astype(jnp.int32).reshape(SECTORS * BLK_DEV, (2 * REACH + 1) * BLK_DEV)


def block_levels(key, dims, cuts, smallest, high):
    def one(dim, shards_of):
        steps = jax.random.uniform(jax.random.fold_in(jax.random.fold_in(key, 6), dim), (shards_of,), jnp.float32, smallest / len(cuts), high / len(cuts))
        return jnp.repeat(jnp.exp(steps), dims[dim] // shards_of).reshape((-1,) + (1,) * (len(dims) - dim - 1))

    factor_of = one(*cuts[0])
    for cut in cuts[1:]:
        factor_of = factor_of * one(*cut)
    return factor_of


def routed_block(key, own, number, rows, amount, top, reach, skew):
    order = jax.random.permutation(key, amount)
    packed, common = load_shares(amount, rows * top, reach, skew, True), load_shares(amount, rows * top, reach, skew, False)
    places = jnp.arange(amount)

    def named(tallies, rotation):
        used = int((tallies > 0).sum())
        fixed = max(1, used // 4)
        moved = fixed + (places - fixed + rotation * (used - fixed)) % max(1, amount - fixed)
        return jnp.zeros((amount,), jnp.int32).at[order[jnp.where(places < fixed, places, moved)]].set(jnp.asarray(tallies, jnp.int32))

    tallies = jnp.where(number % 4 == 0, named(packed, number // 4), named(common, number - number // 4 - 1))
    mixed = jax.random.permutation(jax.random.fold_in(own, 3), amount)
    giver, sink = mixed[0:amount // 2 * 2:2], mixed[1:amount // 2 * 2:2]
    slack = jnp.minimum(tallies[giver] - 1, reach - tallies[sink]) // 2
    slack = jnp.where((giver == order[0]) | (sink == order[0]) | (tallies[sink] == 0), 0, jnp.maximum(slack, 0))
    moved = jax.random.randint(jax.random.fold_in(own, 4), (amount // 2,), 0, 1 << 20) % (slack + 1)
    tallies = tallies.at[giver].add(-moved).at[sink].add(moved)
    labels = jnp.searchsorted(jnp.cumsum(tallies), jnp.arange(rows * top), side="right").astype(jnp.int32)
    table = labels.reshape(top, rows).T
    table = table[jax.random.permutation(jax.random.fold_in(own, 1), rows)]
    rotation = jax.random.randint(jax.random.fold_in(own, 2), (rows, 1), 0, top)
    return jnp.take_along_axis(table, (jnp.arange(top)[None, :] + rotation) % top, axis=1)


def load_shares(count, total, most, skew, full):
    loads = [(1 << 20) // math.isqrt(standing ** skew) + 1 for standing in range(1, count + 1)]
    largest = most if full else min(most, max(-(-total // count), total * loads[0] // sum(loads)))
    least = 1 if total - largest >= count - 1 else 0
    counts, rest = [largest] + [least] * (count - 1), total - largest - least * (count - 1)
    while rest > 0:
        movable = [i for i in range(1, count) if counts[i] < largest] or [i for i in range(1, count) if counts[i] < most]
        pool, left = sum([loads[i] for i in movable]), rest
        for i in movable:
            addition = min(most - counts[i], max(1, left * loads[i] // pool), rest)
            counts[i] = counts[i] + addition
            rest = rest - addition
    return np.array(counts)


def noise(key, dims, spread, reach, pieces=(), held_as=jnp.bfloat16):
    drawn = jax.random.normal(key, dims, jnp.float32) * spread
    if len(pieces) > 0:
        drawn = block_levels(key, dims, pieces, -0.22, 0.18) * drawn
    return jnp.clip(drawn, min=-reach, max=reach).astype(held_as)


def setup_inputs(seed: int = 0) -> dict:
    seeds = jax.random.split(jax.random.key(seed), 10)
    query = draw_query(jax.random.fold_in(seeds[9], 71), 0)
    key = draw_key(jax.random.fold_in(seeds[9], 71), 0)
    value = noise(seeds[2], (HITS, H * HD), 1.0, 6.0, ((0, 128), (1, 2)))
    out_grad = noise(seeds[3], (HITS, H * HD), 8.0, 48.0, ((0, 128), (1, 2)))
    q_weight = noise(seeds[4], (D, H * HD), D ** -0.5, 0.1875, ((1, 2),))
    k_weight = noise(seeds[5], (D, H * HD), D ** -0.5, 0.1875, ((1, 2),))
    v_weight = noise(seeds[6], (D, H * HD), D ** -0.5, 0.1875, ((1, 2),))
    adjacency = draw_adjacency(jax.random.fold_in(seeds[9], 71), 0)
    owner_keys = jax.random.split(jax.random.fold_in(seeds[8], 1), HITS // HITS_DEV)
    owner_turns = jax.random.permutation(jax.random.fold_in(seeds[8], 3), HITS // HITS_DEV)
    owner = jax.vmap(lambda own, number: routed_block(jax.random.fold_in(seeds[8], 2), own, number, HITS_DEV, SECTORS, 1, CAP, 1))(owner_keys, owner_turns).reshape((HITS, 1))
    return {"query": query, "key": key, "value": value, "out_grad": out_grad, "q_weight": q_weight, "k_weight": k_weight, "v_weight": v_weight, "adjacency": adjacency, "owner": owner}


def reference(query, key, value, out_grad, q_weight, k_weight, v_weight, adjacency, owner):
    span_count = 2 * REACH + 1
    factor = 1.0 / math.sqrt(HD)
    q_sect = query.reshape(SECTORS, HITS_DEV, H, HD)
    k_sect = key.reshape(SECTORS, HITS_DEV, H, HD)
    v_sect = value.reshape(SECTORS, HITS_DEV, H, HD)
    g_sect = out_grad.reshape(SECTORS, HITS_DEV, H, HD)
    adj_rows = adjacency.reshape(SECTORS, BLK_DEV, span_count * BLK_DEV)
    row_pos = lax.broadcasted_iota(jnp.int32, (BLK_DEV, span_count * BLK_DEV), 0)
    col_pos = lax.broadcasted_iota(jnp.int32, (BLK_DEV, span_count * BLK_DEV), 1)
    forced = col_pos == REACH * BLK_DEV + row_pos
    offsets = jnp.arange(-REACH, REACH + 1, dtype=jnp.int32)

    def sector_step(carried, sector):
        k_acc, v_acc = carried
        nearby = ((sector + offsets) % SECTORS).astype(jnp.int32)
        k_window = jnp.take(k_sect, nearby, axis=0).reshape(span_count * HITS_DEV, H, HD).astype(jnp.float32)
        v_window = jnp.take(v_sect, nearby, axis=0).reshape(span_count * HITS_DEV, H, HD).astype(jnp.float32)
        allowed = (adj_rows[sector] > 0) | forced
        allowed = jnp.repeat(jnp.repeat(allowed, BLOCK, axis=0), BLOCK, axis=1)
        q_local = q_sect[sector].astype(jnp.float32)
        g_local = g_sect[sector].astype(jnp.float32)
        scores = jnp.einsum('ihd,jhd->hij', q_local, k_window) * factor
        masked = jnp.where(allowed[None], scores, -jnp.inf)
        row_top = lax.optimization_barrier(jnp.max(masked, axis=2, keepdims=True))
        log_total = row_top + jnp.log(lax.optimization_barrier(jnp.sum(jnp.exp(masked - row_top), axis=2, keepdims=True)))
        prob = jnp.where(allowed[None], jnp.exp(scores - log_total), 0.0)
        prob_low = lax.optimization_barrier(prob.astype(jnp.bfloat16)).astype(jnp.float32)
        attended = jnp.einsum('hij,jhd->ihd', prob_low, v_window)
        row_delta = lax.optimization_barrier(jnp.sum(g_local * attended, axis=2))
        prob_grad = jnp.einsum('ihd,jhd->hij', g_local, v_window)
        score_grad = prob * (prob_grad - jnp.transpose(row_delta)[:, :, None])
        score_grad = lax.optimization_barrier(score_grad.astype(jnp.bfloat16)).astype(jnp.float32)
        q_rows = (jnp.einsum('hij,jhd->ihd', score_grad, k_window) * factor).reshape(HITS_DEV, H * HD).astype(jnp.bfloat16)
        k_terms = (jnp.einsum('hij,ihd->jhd', score_grad, q_local) * factor).reshape(span_count, HITS_DEV, H * HD)
        k_terms = lax.optimization_barrier(k_terms.astype(jnp.bfloat16)).astype(jnp.float32)
        v_terms = jnp.einsum('hij,ihd->jhd', prob_low, g_local).reshape(span_count, HITS_DEV, H * HD)
        v_terms = lax.optimization_barrier(v_terms.astype(jnp.bfloat16)).astype(jnp.float32)
        k_acc = k_acc.at[nearby].add(k_terms)
        v_acc = v_acc.at[nearby].add(v_terms)
        return ((k_acc, v_acc), q_rows)
    empty = jnp.zeros((SECTORS, HITS_DEV, H * HD), jnp.float32)
    (k_acc, v_acc), q_rows = lax.scan(sector_step, (empty, empty), jnp.arange(SECTORS, dtype=jnp.int32))
    q_grad = q_rows.reshape(HITS, H * HD)
    k_grad = k_acc.reshape(HITS, H * HD).astype(jnp.bfloat16)
    v_grad = v_acc.reshape(HITS, H * HD).astype(jnp.bfloat16)
    input_grad = jnp.dot(q_grad, q_weight.T, preferred_element_type=jnp.float32)
    input_grad = input_grad + jnp.dot(k_grad, k_weight.T, preferred_element_type=jnp.float32)
    input_grad = input_grad + jnp.dot(v_grad, v_weight.T, preferred_element_type=jnp.float32)
    input_grad = input_grad.astype(jnp.bfloat16)
    owners = owner.reshape(SECTORS, HITS_DEV)
    earlier = lax.broadcasted_iota(jnp.int32, (HITS_DEV, HITS_DEV), 0) > lax.broadcasted_iota(jnp.int32, (HITS_DEV, HITS_DEV), 1)
    same_dest = owners[:, :, None] == owners[:, None, :]
    slot_rank = lax.optimization_barrier(jnp.sum((same_dest & earlier[None]).astype(jnp.int32), axis=2)).astype(jnp.int32)
    sources = jnp.arange(SECTORS, dtype=jnp.int32)[:, None]
    targets = (owners * (SECTORS * CAP) + sources * CAP + slot_rank).reshape(-1).astype(jnp.int32)
    return jnp.zeros((SECTORS * SECTORS * CAP, D), jnp.bfloat16).at[targets].set(input_grad)
```

```python
import functools
import math

import jax
import jax.numpy as jnp
from jax import lax
from jax.experimental import pallas as pl
from jax.experimental.pallas import tpu as pltpu
from jax.sharding import PartitionSpec as P

HD = 64
BLOCK = 128
REACH = 3
SPAN = 2 * REACH + 1
LOG2E = math.log2(math.e)
MASKED = -1e30
BF = jnp.bfloat16
F32 = jnp.float32
NT = (((1,), (1,)), ((), ()))
NN = (((1,), (0,)), ((), ()))
TN = (((0,), (0,)), ((), ()))
PARAMS = dict(vmem_limit_bytes=48 << 20)


def dot(a, b, dims):
    return lax.dot_general(a, b, dims, preferred_element_type=F32)


def moved(value, steps):
    count = lax.axis_size("blk")
    return lax.ppermute(value, "blk", [(s, (s + steps) % count) for s in range(count)])


def core_swapped(value):
    count = lax.axis_size("blk")
    return lax.ppermute(value, "blk", [(s, s ^ 1) for s in range(count)])


def bias_rows(adj_ref):
    shape = (16, 2 * BLOCK)
    row = lax.broadcasted_iota(jnp.int32, shape, 0)
    query_block = lax.broadcasted_iota(jnp.int32, shape, 1) // BLOCK
    allowed = row == 2 * REACH + query_block
    for c in range(2 * SPAN):
        for b in range(2):
            hit = (row == c) & (query_block == b) & (adj_ref[b, c] > 0)
            allowed = allowed | hit
    return jnp.where(allowed, 0.0, MASKED)


def pack_kernel(par_ref, adj_ref, q_ref, k_ref, v_ref, g_ref, send_ref):
    rows, cols = q_ref.shape
    send_ref[0:rows, 0:cols] = k_ref[...]
    send_ref[0:rows, cols : 2 * cols] = v_ref[...]
    send_ref[0:rows, 2 * cols : 3 * cols] = q_ref[...]
    send_ref[0:rows, 3 * cols : 4 * cols] = g_ref[...]
    send_ref[rows : rows + 16, 0:cols] = bias_rows(adj_ref).astype(BF)
    send_ref[rows : rows + 16, cols:] = jnp.zeros((16, 3 * cols), BF)


def order_kernel(par_ref, adj_ref, q_ref, k_ref, v_ref, g_ref, got_ref, kv_ref, first_ref, second_ref, qg_ref, bias_ref):
    rows, cols = q_ref.shape
    par = par_ref[0]
    other = 1 - par
    kv_ref[0, par] = k_ref[...]
    kv_ref[1, par] = v_ref[...]
    qg_ref[0, par] = q_ref[...] * (1.0 / math.sqrt(HD))
    qg_ref[1, par] = g_ref[...]
    kv_ref[0, other] = got_ref[0:rows, 0:cols]
    kv_ref[1, other] = got_ref[0:rows, cols : 2 * cols]
    qg_ref[0, other] = got_ref[0:rows, 2 * cols : 3 * cols] * (1.0 / math.sqrt(HD))
    qg_ref[1, other] = got_ref[0:rows, 3 * cols : 4 * cols]
    bias_ref[par] = bias_rows(adj_ref)
    bias_ref[other] = got_ref[rows : rows + 16, 0:cols].astype(F32)
    first_ref[...] = kv_ref[:, 0]
    second_ref[...] = kv_ref[:, 1]


def attention_kernel(
    par_ref, left2_ref, left_ref, mid_ref, right_ref, right2_ref, qg_ref, bias_ref,
    dleft2_ref, dleft_ref, dmid_ref, dright_ref, dright2_ref, dq_own_ref, dq_send_ref,
    s_ref, d_ref, p_ref, ds_ref, qs_ref, gs_ref,
):
    rows = qg_ref.shape[2]
    lanes = qg_ref.shape[3]

    def window(which, w):
        if w == 0:
            return left2_ref[which]
        if w < 3:
            return left_ref[which, w - 1]
        if w < 5:
            return mid_ref[which, w - 3]
        if w < 7:
            return right_ref[which, w - 5]
        return right2_ref[which]

    lane_head = lax.broadcasted_iota(jnp.int32, (rows, lanes), 1) // HD
    for t in range(2):
        for h in range(2):
            block = t * 2 + h
            cols = slice(block * rows, (block + 1) * rows)
            qh = jnp.where(lane_head == h, qg_ref[0, t], 0.0).astype(BF)
            gh = jnp.where(lane_head == h, qg_ref[1, t], 0.0).astype(BF)
            qs_ref[cols, :] = qh
            gs_ref[cols, :] = gh
            top = None
            for j in range(SPAN):
                scores = dot(window(0, t + j), qh, NT)
                s_ref[j * rows : (j + 1) * rows, :] = scores
                for b in range(2):
                    c = 2 * j + b
                    block_top = jnp.max(scores[b * BLOCK : (b + 1) * BLOCK], axis=0, keepdims=True)
                    block_top = block_top + bias_ref[t, c : c + 1, :]
                    top = block_top if top is None else jnp.maximum(top, block_top)
            total = jnp.zeros((1, rows), F32)
            delta = jnp.zeros((1, rows), F32)
            for j in range(SPAN):
                grads = dot(window(1, t + j), gh, NT)
                d_ref[j * rows : (j + 1) * rows, :] = grads
                for b in range(2):
                    c = 2 * j + b
                    at = slice(j * rows + b * BLOCK, j * rows + (b + 1) * BLOCK)
                    shift = (bias_ref[t, c : c + 1, :] - top) * LOG2E
                    weight = jnp.exp2(s_ref[at, :] * LOG2E + shift)
                    s_ref[at, :] = weight
                    total = total + jnp.sum(weight, axis=0, keepdims=True)
                    delta = delta + jnp.sum(
                        weight * grads[b * BLOCK : (b + 1) * BLOCK], axis=0, keepdims=True
                    )
            scale = 1.0 / total
            delta = delta * scale
            for j in range(SPAN):
                at = slice(j * rows, (j + 1) * rows)
                to = slice((t + j) * rows, (t + j + 1) * rows)
                prob = s_ref[at, :] * scale
                p_ref[to, cols] = prob.astype(BF)
                ds_ref[to, cols] = (prob * (d_ref[at, :] - delta)).astype(BF)
    for w in range(SPAN + 1):
        low = 0 if w < SPAN else 2 * rows
        high = 4 * rows if w > 0 else 2 * rows
        at = slice(w * rows, (w + 1) * rows)
        for which, (left_operand, right_operand) in enumerate(((ds_ref, qs_ref), (p_ref, gs_ref))):
            term = dot(left_operand[at, low:high], right_operand[low:high, :], NN)
            if w == 0:
                dleft2_ref[which] = term.astype(BF)
            elif w < 3:
                dleft_ref[which, w - 1] = term.astype(BF)
            elif w < 5:
                dmid_ref[which, w - 3] = term
            elif w < 7:
                dright_ref[which, w - 5] = term.astype(BF)
            else:
                dright2_ref[which] = term.astype(BF)
    sector_grads = []
    for t in range(2):
        parts = []
        for h in range(2):
            block = t * 2 + h
            acc = None
            for j in range(SPAN):
                w = t + j
                part = dot(ds_ref[w * rows : (w + 1) * rows, block * rows : (block + 1) * rows], window(0, w), TN)
                acc = part if acc is None else acc + part
            parts.append(acc)
        sector_grads.append(jnp.where(lane_head == 0, parts[0], parts[1]) * (1.0 / math.sqrt(HD)))
    first = par_ref[0] == 0
    dq_own_ref[...] = jnp.where(first, sector_grads[0], sector_grads[1]).astype(BF)
    dq_send_ref[...] = jnp.where(first, sector_grads[1], sector_grads[0]).astype(BF)


def total_kernel(par_ref, mid_ref, right_ref, left_ref, right2_ref, left2_ref, keep_ref, send_ref):
    par = par_ref[0]
    other = 1 - par
    first = par == 0
    for which in range(2):
        far0 = left2_ref[which].astype(F32)
        far1 = right2_ref[which].astype(F32)
        for sector, out_ref in ((par, keep_ref), (other, send_ref)):
            far = jnp.where(first, far0, far1) if out_ref is keep_ref else jnp.where(first, far1, far0)
            value = mid_ref[which, sector] + right_ref[which, sector].astype(F32)
            value = value + left_ref[which, sector].astype(F32) + far
            out_ref[which] = value.astype(BF)


def project_kernel(par_ref, dq_ref, dq2_ref, dkv_ref, dkv2_ref, wq_ref, wk_ref, wv_ref, out_ref):
    first = par_ref[0] == 0
    half = dq_ref.shape[1]
    total = None
    for own, got, weight in (
        (dq_ref[...], dq2_ref[...], wq_ref),
        (dkv_ref[0], dkv2_ref[0], wk_ref),
        (dkv_ref[1], dkv2_ref[1], wv_ref),
    ):
        low = jnp.where(first, own, got)
        high = jnp.where(first, got, own)
        term = dot(low, weight[:, 0:half], NT) + dot(high, weight[:, half:], NT)
        total = term if total is None else total + term
    out_ref[...] = total.astype(out_ref.dtype)


def route_kernel(owner_col_ref, owner_row_ref, place_ref):
    rows = owner_col_ref.shape[0]
    slots = place_ref.shape[0]
    owner_row = owner_row_ref[...]
    earlier = lax.broadcasted_iota(jnp.int32, (rows, rows), 0) < lax.broadcasted_iota(jnp.int32, (rows, rows), 1)
    same = (owner_col_ref[...] == owner_row) & earlier
    rank = jnp.sum(same.astype(jnp.int32), axis=0, keepdims=True)
    target = owner_row * 4 + rank
    slot = lax.broadcasted_iota(jnp.int32, (slots, rows), 0)
    place_ref[...] = jnp.where(slot == target, 1.0, 0.0).astype(BF)


def scatter_kernel(own_ref, got_ref, place_ref, out_ref):
    value = (own_ref[...] + got_ref[...].astype(F32)).astype(BF)
    out_ref[...] = dot(place_ref[...], value, NN).astype(BF)


def cost(flops, moved_bytes, exps=0):
    return pl.CostEstimate(flops=flops, bytes_accessed=moved_bytes, transcendentals=exps)


def on_device(query, key, value, out_grad, q_weight, k_weight, v_weight, adjacency, owner):
    rows, cols = query.shape
    half = cols // 2
    pair = 2 * HD
    sds = jax.ShapeDtypeStruct
    par = jnp.reshape(lax.axis_index("blk") % 2, (1,)).astype(jnp.int32)
    head = jnp.reshape(lax.axis_index("head"), (1,)).astype(jnp.int32)
    smem = pl.BlockSpec(memory_space=pltpu.SMEM)
    vmem = pl.BlockSpec(memory_space=pltpu.VMEM)

    def call(kernel, outs, grid, in_specs, out_specs, scratch=(), scalars=1, estimate=None):
        return pl.pallas_call(
            kernel,
            out_shape=outs,
            grid_spec=pltpu.PrefetchScalarGridSpec(
                num_scalar_prefetch=scalars, grid=grid, in_specs=in_specs, out_specs=out_specs,
                scratch_shapes=list(scratch),
            ),
            compiler_params=pltpu.CompilerParams(**PARAMS),
            cost_estimate=estimate,
        )

    own_half = pl.BlockSpec((rows, half), lambda i, p: (0, p[0]))
    other_half = pl.BlockSpec((rows, half), lambda i, p: (0, 1 - p[0]))

    def whole(*shape):
        return pl.BlockSpec(shape, lambda i, p: (0,) * len(shape))

    send = call(
        pack_kernel, sds((rows + 16, 4 * half), BF), (1,), [smem] + [other_half] * 4, whole(rows + 16, 4 * half)
    )(par, adjacency, query, key, value, out_grad)
    got = core_swapped(send)
    kv, kv_first, kv_second, qg, bias = call(
        order_kernel,
        (
            sds((2, 2, rows, half), BF),
            sds((2, rows, half), BF),
            sds((2, rows, half), BF),
            sds((2, 2, rows, half), BF),
            sds((2, 16, rows), F32),
        ),
        (1,),
        [smem] + [own_half] * 4 + [whole(rows + 16, 4 * half)],
        (whole(2, 2, rows, half), whole(2, rows, half), whole(2, rows, half), whole(2, 2, rows, half), whole(2, 16, rows)),
    )(par, adjacency, query, key, value, out_grad, got)
    from_left = moved(kv, 2)
    from_right = moved(kv, -2)
    from_left2 = moved(kv_second, 4)
    from_right2 = moved(kv_first, -4)

    slots = 4 * lax.axis_size("blk")
    place = pl.pallas_call(
        route_kernel, out_shape=sds((slots, rows), BF), in_specs=[vmem, vmem], out_specs=vmem
    )(owner, owner.reshape(1, rows))

    near = pl.BlockSpec((2, 2, rows, pair), lambda i, p: (0, 0, 0, i))
    far = pl.BlockSpec((2, rows, pair), lambda i, p: (0, 0, i))
    dq_spec = pl.BlockSpec((rows, pair), lambda i, p: (0, i))
    big = (SPAN + 1) * rows
    dleft2, dleft, dmid, dright, dright2, dq_own, dq_send = call(
        attention_kernel,
        (
            sds((2, rows, half), BF),
            sds((2, 2, rows, half), BF),
            sds((2, 2, rows, half), F32),
            sds((2, 2, rows, half), BF),
            sds((2, rows, half), BF),
            sds((rows, half), BF),
            sds((rows, half), BF),
        ),
        (half // pair,),
        [far, near, near, near, far, near, whole(2, 16, rows)],
        (far, near, near, near, far, dq_spec, dq_spec),
        scratch=(
            pltpu.VMEM((SPAN * rows, rows), F32),
            pltpu.VMEM((SPAN * rows, rows), F32),
            pltpu.VMEM((big, 4 * rows), BF),
            pltpu.VMEM((big, 4 * rows), BF),
            pltpu.VMEM((4 * rows, pair), BF),
            pltpu.VMEM((4 * rows, pair), BF),
        ),
    )(par, from_left2, from_left, kv, from_right, from_right2, qg, bias)
    got_right = moved(dleft, -2)
    got_left = moved(dright, 2)
    got_right2 = moved(dleft2, -4)
    got_left2 = moved(dright2, 4)
    dq_got = core_swapped(dq_send)
    keep, give = call(
        total_kernel,
        (sds((2, rows, half), BF), sds((2, rows, half), BF)),
        (1,),
        [whole(2, 2, rows, half)] * 3 + [whole(2, rows, half)] * 2,
        (whole(2, rows, half), whole(2, rows, half)),
    )(par, dmid, got_right, got_left, got_right2, got_left2)
    gave = core_swapped(give)

    scalars = jnp.concatenate([par, head])
    weight_other = pl.BlockSpec((cols, cols), lambda i, p: (1 - p[1], 0))
    weight_own = pl.BlockSpec((cols, cols), lambda i, p: (p[1], 0))
    terms = [whole(rows, half)] * 2 + [whole(2, rows, half)] * 2
    operands = (scalars, dq_own, dq_got, keep, gave, q_weight, k_weight, v_weight)
    partial_other = call(
        project_kernel, sds((rows, cols), BF), (1,), terms + [weight_other] * 3, whole(rows, cols)
    )(*operands)
    partial_got = lax.ppermute(partial_other, "head", [(0, 1), (1, 0)])
    partial_own = call(
        project_kernel, sds((rows, cols), F32), (1,), terms + [weight_own] * 3, whole(rows, cols)
    )(*operands)
    outgoing = pl.pallas_call(
        scatter_kernel, out_shape=sds((slots, cols), BF), in_specs=[vmem] * 3, out_specs=vmem
    )(partial_own, partial_got, place)
    return lax.all_to_all(outgoing, "blk", split_axis=0, concat_axis=0, tiled=True)


def solution(mesh):
    return jax.shard_map(
        on_device,
        mesh=mesh,
        in_specs=(
            P("blk", "head"),
            P("blk", "head"),
            P("blk", "head"),
            P("blk", "head"),
            P(None, "head"),
            P(None, "head"),
            P(None, "head"),
            P("blk", None),
            P("blk", None),
        ),
        out_specs=P("blk", "head"),
        check_vma=False,
    )
```

```python
import functools
import math

import jax
import jax.numpy as jnp
import numpy as np
from jax import lax
from jax.experimental import pallas as pl
from jax.experimental.pallas import tpu as pltpu
from jax.sharding import PartitionSpec as P

HD = 64
BLOCK = 128
REACH = 3
SPAN = 2 * REACH + 1
LOG2E = math.log2(math.e)
MASKED = -1e30
FLOOR = -1e29
CAP = 4
BF = jnp.bfloat16
F32 = jnp.float32
NT = (((1,), (1,)), ((), ()))
NN = (((1,), (0,)), ((), ()))
TN = (((0,), (0,)), ((), ()))


def dot(a, b, dims):
    return lax.dot_general(a, b, dims, preferred_element_type=F32)


def core_swapped(value):
    count = lax.axis_size("blk")
    return lax.ppermute(value, "blk", [(s, s ^ 1) for s in range(count)])


def chip_swapped(value, odd):
    count = lax.axis_size("blk")
    ahead = [2 if (s // 2) % 2 == odd else -2 for s in range(count)]
    return lax.ppermute(value, "blk", [(s, (s + ahead[s]) % count) for s in range(count)])


def bias_rows(adj_ref):
    shape = (16, 2 * BLOCK)
    row = lax.broadcasted_iota(jnp.int32, shape, 0)
    query_block = lax.broadcasted_iota(jnp.int32, shape, 1) // BLOCK
    allowed = row == 2 * REACH + query_block
    for c in range(2 * SPAN):
        for b in range(2):
            hit = (row == c) & (query_block == b) & (adj_ref[b, c] > 0)
            allowed = allowed | hit
    return jnp.where(allowed, 0.0, MASKED)


def pack_kernel(ids_ref, adj_ref, k_ref, v_ref, q_ref, g_ref, send_ref, own_ref, sems):
    rows, cols = k_ref.shape
    half = cols // 2
    copies = []
    for to_ref, which in ((send_ref, 1 - ids_ref[0]), (own_ref, ids_ref[0])):
        at = pl.ds(pl.multiple_of(which * half, half), half)
        for n, from_ref in enumerate((k_ref, v_ref, q_ref, g_ref)):
            copies.append(
                pltpu.make_async_copy(
                    from_ref.at[:, at], to_ref.at[0:rows, n * half : (n + 1) * half], sems.at[len(copies)]
                )
            )
    for copy in copies:
        copy.start()
    bias = bias_rows(adj_ref).astype(BF)
    for to_ref in (send_ref, own_ref):
        to_ref[rows : rows + 16, 0:half] = bias
        to_ref[rows : rows + 16, half:] = jnp.zeros((16, 3 * half), BF)
    for copy in copies:
        copy.wait()


def order_kernel(ids_ref, own_ref, got_ref, a_ref, b_ref, qg_ref, bias_ref):
    rows = a_ref.shape[1]
    cols = a_ref.shape[2]
    par = ids_ref[0]
    scale = 1.0 / math.sqrt(HD)
    for sector, from_ref in ((par, own_ref), (1 - par, got_ref)):
        qg_ref[0, sector] = from_ref[0:rows, 2 * cols : 3 * cols] * scale
        qg_ref[1, sector] = from_ref[0:rows, 3 * cols : 4 * cols]
        bias_ref[sector] = from_ref[rows : rows + 16, 0:cols].astype(F32)
    b_own = par == ids_ref[1]
    for which in range(2):
        own = own_ref[0:rows, which * cols : (which + 1) * cols]
        got = got_ref[0:rows, which * cols : (which + 1) * cols]
        a_ref[which] = jnp.where(b_own, got, own)
        b_ref[which] = jnp.where(b_own, own, got)


def one_head(pair_ref, h):
    value = pair_ref[...]
    lane_head = lax.broadcasted_iota(jnp.int32, value.shape, 1) // HD
    return jnp.where(lane_head == h, value, 0.0).astype(BF)


def bias_pair_of(bias_ref, t, j):
    return [bias_ref[t, pl.ds(2 * j + b, 1), :] for b in range(2)]


def fold_stats(stats, key_value, query_head, grad_head, bias_pair):
    scores = dot(key_value[0], query_head, NT)
    grads = dot(key_value[1], grad_head, NT)
    top, total, delta = stats
    for b in range(2):
        at = slice(b * BLOCK, (b + 1) * BLOCK)
        new_top = jnp.maximum(top, jnp.max(scores[at], axis=0, keepdims=True) + bias_pair[b])
        weight = jnp.exp2(scores[at] * LOG2E + (bias_pair[b] - new_top) * LOG2E)
        shrink = jnp.exp2((top - new_top) * LOG2E)
        total = jnp.sum(weight, axis=0, keepdims=True) + total * shrink
        delta = jnp.sum(weight * grads[at], axis=0, keepdims=True) + delta * shrink
        top = new_top
    return (top, total, delta), scores, grads


def near_stats_kernel(ids_ref, *refs):
    windows = refs[0:6]
    qg_ref, bias_ref, stats_ref = refs[6:9]
    odd = ids_ref[1]
    names = (4 - odd, 3 + odd, 5 - 3 * odd, 2 + 3 * odd, 6 - 5 * odd, 1 + 5 * odd)
    rows = qg_ref.shape[2]
    for t in range(2):
        for h in range(2):
            qh = one_head(qg_ref.at[0, t], h)
            gh = one_head(qg_ref.at[1, t], h)
            zero = jnp.zeros((1, rows), F32)
            stats = (zero + FLOOR, zero, zero)
            for w, window in zip(names, windows):
                stats, _, _ = fold_stats(stats, window, qh, gh, bias_pair_of(bias_ref, t, w - t))
            for row in range(3):
                stats_ref[t, h, row : row + 1, :] = stats[row]


def head_rows_of(first, second):
    row_head = lax.broadcasted_iota(jnp.int32, first.shape, 0) // HD
    return jnp.where(row_head == 0, first, second)


def query_grad(keys_t, grads, rows):
    both = dot(keys_t, grads, NN)
    return head_rows_of(both[:, 0:rows], both[:, rows:])


def flipped(value):
    return jnp.transpose(value.astype(F32)).astype(BF)


def far_kernel(
    ids_ref, e_ref, o_ref, qg_ref, bias_ref, stats_ref, final_ref, de_ref, do_ref, dq_ref,
    ps_ref, ds_ref, qs_ref, gs_ref,
):
    rows = qg_ref.shape[2]
    odd = ids_ref[1]
    for n, (t, window, out_ref) in enumerate(((1 - odd, e_ref, de_ref), (odd, o_ref, do_ref))):
        for h in range(2):
            cols = slice(h * rows, (h + 1) * rows)
            qh = one_head(qg_ref.at[0, t], h)
            gh = one_head(qg_ref.at[1, t], h)
            qs_ref[n, cols, :] = qh
            gs_ref[n, cols, :] = gh
            bias_pair = bias_pair_of(bias_ref, t, (SPAN - 1) * t)
            stats = tuple(stats_ref[t, h, row : row + 1, :] for row in range(3))
            (top, total, delta), scores, grads = fold_stats(stats, window, qh, gh, bias_pair)
            log_total = top * LOG2E + jnp.log2(total)
            delta = delta / total
            final_ref[t, h, 0:1, :] = log_total
            final_ref[t, h, 1:2, :] = delta
            for b in range(2):
                at = slice(b * BLOCK, (b + 1) * BLOCK)
                prob = jnp.exp2(scores[at] * LOG2E + (bias_pair[b] * LOG2E - log_total))
                ps_ref[n, at, cols] = prob.astype(BF)
                ds_ref[n, at, cols] = (prob * (grads[at] - delta)).astype(BF)
        out_ref[0] = dot(ds_ref[n], qs_ref[n], NN).astype(BF)
        out_ref[1] = dot(ps_ref[n], gs_ref[n], NN).astype(BF)
        dq_ref[0, t] = query_grad(flipped(window[0]), ds_ref[n], rows)


def shared_kernel(names, qg_ref, bias_ref, final_ref, windows, outs, ps_ref, ds_ref, qs_ref, gs_ref, kt_ref):
    rows = qg_ref.shape[2]
    for t in range(2):
        for h in range(2):
            block = 2 * t + h
            cols = slice(block * rows, (block + 1) * rows)
            qs_ref[cols, :] = one_head(qg_ref.at[0, t], h)
            gs_ref[cols, :] = one_head(qg_ref.at[1, t], h)
    for n, (w, window) in enumerate(zip(names, windows)):
        keys = slice(n * rows, (n + 1) * rows)
        kt_ref[:, keys] = flipped(window[0])
        for t in range(2):
            for h in range(2):
                block = 2 * t + h
                cols = slice(block * rows, (block + 1) * rows)
                scores = dot(window[0], qs_ref[cols, :], NT)
                grads = dot(window[1], gs_ref[cols, :], NT)
                log_total = final_ref[t, h, 0:1, :]
                delta = final_ref[t, h, 1:2, :]
                bias_pair = bias_pair_of(bias_ref, t, w - t)
                for b in range(2):
                    at = slice(b * BLOCK, (b + 1) * BLOCK)
                    to = slice(n * rows + b * BLOCK, n * rows + (b + 1) * BLOCK)
                    prob = jnp.exp2(scores[at] * LOG2E + (bias_pair[b] * LOG2E - log_total))
                    ps_ref[to, cols] = prob.astype(BF)
                    ds_ref[to, cols] = (prob * (grads[at] - delta)).astype(BF)
        out_ref = outs[n]
        out_ref[0] = dot(ds_ref[keys, :], qs_ref[...], NN).astype(out_ref.dtype)
        out_ref[1] = dot(ps_ref[keys, :], gs_ref[...], NN).astype(out_ref.dtype)
    return [
        query_grad(kt_ref[...], ds_ref[:, 2 * t * rows : 2 * (t + 1) * rows], rows) for t in range(2)
    ]


def near_kernel(ids_ref, ea_ref, oa_ref, eb_ref, ob_ref, qg_ref, bias_ref, final_ref, part_ref, *refs):
    outs, dq_ref, scratch = refs[0:4], refs[4], refs[5:]
    odd = ids_ref[1]
    names = (5 - 3 * odd, 2 + 3 * odd, 6 - 5 * odd, 1 + 5 * odd)
    grads = shared_kernel(names, qg_ref, bias_ref, final_ref, (ea_ref, oa_ref, eb_ref, ob_ref), outs, *scratch)
    for t in range(2):
        dq_ref[0, t] = part_ref[0, t] + grads[t]


def local_kernel(ids_ref, a_ref, b_ref, qg_ref, bias_ref, final_ref, part_ref, *refs):
    outs, (dq_own_ref, dq_send_ref), scratch = refs[0:2], refs[2:4], refs[4:]
    odd = ids_ref[1]
    grads = shared_kernel((4 - odd, 3 + odd), qg_ref, bias_ref, final_ref, (a_ref, b_ref), outs, *scratch)
    total = [part_ref[0, t] + grads[t] for t in range(2)]
    first = ids_ref[0] == 0
    scale = 1.0 / math.sqrt(HD)
    dq_own_ref[...] = jnp.transpose(jnp.where(first, total[0], total[1]) * scale).astype(BF)
    dq_send_ref[...] = jnp.transpose(jnp.where(first, total[1], total[0]) * scale).astype(BF)


def joined(first, second):
    return (first.astype(F32) + second.astype(F32)).astype(BF)


def total_kernel(ids_ref, a_ref, b_ref, ea_ref, oa_ref, eb_ref, ob_ref, keep_ref, send_ref):
    b_own = ids_ref[0] == ids_ref[1]
    for which in range(2):
        value_a = a_ref[which] + ob_ref[which].astype(F32) + ea_ref[which].astype(F32)
        value_b = b_ref[which] + eb_ref[which].astype(F32) + oa_ref[which].astype(F32)
        keep_ref[which] = jnp.where(b_own, value_b, value_a).astype(BF)
        send_ref[which] = jnp.where(b_own, value_a, value_b).astype(BF)


def query_kernel(ids_ref, own_ref, got_ref, weight_ref, other_out_ref, own_out_ref):
    first = ids_ref[0] == 0
    half = own_ref.shape[1]
    low = jnp.where(first, own_ref[...], got_ref[...])
    high = jnp.where(first, got_ref[...], own_ref[...])
    cols = own_out_ref.shape[1]
    here = ids_ref[2]
    for out_ref, which in ((other_out_ref, 1 - here), (own_out_ref, here)):
        at = pl.ds(pl.multiple_of(which * cols, cols), cols)
        out_ref[...] = dot(low, weight_ref[at, 0:half], NT) + dot(high, weight_ref[at, half:], NT)


def add_kernel(ids_ref, base_ref, grads_ref, wk_ref, wv_ref, out_ref):
    value = base_ref[...] + dot(grads_ref[0], wk_ref[...], NT) + dot(grads_ref[1], wv_ref[...], NT)
    out_ref[...] = value.astype(out_ref.dtype)


def both_kernel(ids_ref, base_ref, keep_ref, gave_ref, wk_ref, wv_ref, out_ref):
    first = ids_ref[0] == 0
    half = keep_ref.shape[2]
    value = base_ref[...]
    for which, weight in ((0, wk_ref), (1, wv_ref)):
        low = jnp.where(first, keep_ref[which], gave_ref[which])
        high = jnp.where(first, gave_ref[which], keep_ref[which])
        value = value + dot(low, weight[:, 0:half], NT) + dot(high, weight[:, half:], NT)
    out_ref[...] = value


def route_kernel(owner_col_ref, owner_row_ref, label_ref, place_ref):
    rows = owner_col_ref.shape[0]
    owner_row = owner_row_ref[...]
    earlier = lax.broadcasted_iota(jnp.int32, (rows, rows), 0) < lax.broadcasted_iota(jnp.int32, (rows, rows), 1)
    same = (owner_col_ref[...] == owner_row) & earlier
    rank = jnp.sum(same.astype(jnp.int32), axis=0, keepdims=True)
    target = owner_row * CAP + rank
    place_ref[...] = jnp.where(label_ref[...] == target, 1.0, 0.0).astype(BF)


def scatter_kernel(own_ref, got_ref, place_ref, out_ref):
    value = (own_ref[...] + got_ref[...].astype(F32)).astype(BF)
    out_ref[...] = dot(place_ref[...], value, NN).astype(BF)


def spread_order(count):
    groups = [int(g) for g in np.random.default_rng(1).permutation(count // 4)]
    return [4 * g + i for g in groups for i in range(4)]


def restore_kernel(from_ref, out_ref, *, home):
    rows = out_ref.shape[0] // len(home)
    for i, g in enumerate(home):
        out_ref[i * rows : (i + 1) * rows, :] = from_ref[g * rows : (g + 1) * rows, :]


def cost(flops, moved_bytes, exps=0):
    return pl.CostEstimate(flops=flops, bytes_accessed=moved_bytes, transcendentals=exps)


def on_device(query, key, value, out_grad, q_weight, k_weight, v_weight, adjacency, owner):
    rows, cols = query.shape
    half = cols // 2
    pair = 2 * HD
    sds = jax.ShapeDtypeStruct
    block = lax.axis_index("blk")
    ids = jnp.stack([block % 2, (block // 2) % 2, lax.axis_index("head")]).astype(jnp.int32)
    smem = pl.BlockSpec(memory_space=pltpu.SMEM)
    hbm = pl.BlockSpec(memory_space=pltpu.HBM)

    def call(kernel, outs, grid, in_specs, out_specs, scratch=(), scalars=1, estimate=None, limit=16):
        return pl.pallas_call(
            kernel,
            out_shape=outs,
            grid_spec=pltpu.PrefetchScalarGridSpec(
                num_scalar_prefetch=scalars, grid=grid, in_specs=in_specs, out_specs=out_specs,
                scratch_shapes=list(scratch),
            ),
            compiler_params=pltpu.CompilerParams(vmem_limit_bytes=limit << 20),
            cost_estimate=estimate,
        )

    def whole(*shape):
        return pl.BlockSpec(shape, lambda i, *p: (0,) * len(shape))

    packed = sds((rows + 16, 4 * half), BF)
    send, own = call(
        pack_kernel, (packed, packed), (1,), [smem] + [hbm] * 4, (whole(rows + 16, 4 * half),) * 2,
        scratch=(pltpu.SemaphoreType.DMA((8,)),), limit=60,
    )(ids, adjacency, key, value, query, out_grad)
    got = core_swapped(send)
    kv_shape = sds((2, rows, half), BF)
    kv_whole = whole(2, rows, half)
    a, b, qg, bias = call(
        order_kernel,
        (kv_shape, kv_shape, sds((2, 2, rows, half), BF), sds((2, 16, rows), F32)),
        (1,),
        [whole(rows + 16, 4 * half)] * 2,
        (kv_whole, kv_whole, whole(2, 2, rows, half), whole(2, 16, rows)),
    )(ids, own, got)
    ea = chip_swapped(a, 0)
    oa = chip_swapped(b, 1)
    eb = chip_swapped(b, 0)
    ob = chip_swapped(a, 1)
    ef = chip_swapped(oa, 0)
    of = chip_swapped(ea, 1)

    count = lax.axis_size("blk")
    slots = CAP * count
    order = spread_order(count)
    labels = jnp.asarray(np.array([[CAP * s + r] for s in order for r in range(CAP)], np.int32))
    place = call(
        route_kernel, sds((slots, rows), BF), (1,),
        [whole(rows, 1), whole(1, rows), whole(slots, 1)], whole(slots, rows), scalars=0,
        estimate=cost(rows * rows * 8, 1 << 20),
    )(owner, owner.reshape(1, rows), labels)

    pairs = half // pair
    win = pl.BlockSpec((2, rows, pair), lambda i, p: (0, 0, i))
    near = pl.BlockSpec((2, 2, rows, pair), lambda i, p: (0, 0, 0, i))
    dq_spec = pl.BlockSpec((rows, pair), lambda i, p: (0, i))
    stat_spec = pl.BlockSpec((2, 2, 8, rows), lambda i, p: (0, i, 0, 0))
    bias_spec = whole(2, 16, rows)
    stat_shape = sds((2, 2 * pairs, 8, rows), F32)
    step = 2 * rows * rows * HD * 4
    part_shape = sds((pairs, 2, pair, rows), F32)
    part_spec = pl.BlockSpec((1, 2, pair, rows), lambda i, p: (i, 0, 0, 0))

    def scratch(blocks):
        return (
            pltpu.VMEM((blocks * rows, 4 * rows), BF),
            pltpu.VMEM((blocks * rows, 4 * rows), BF),
            pltpu.VMEM((4 * rows, pair), BF),
            pltpu.VMEM((4 * rows, pair), BF),
            pltpu.VMEM((pair, blocks * rows), BF),
        )

    stats = call(
        near_stats_kernel, stat_shape, (pairs,), [win] * 6 + [near, bias_spec], stat_spec,
        estimate=cost(24 * step, 6 << 20),
    )(ids, a, b, ea, oa, eb, ob, qg, bias)
    stats, place = lax.optimization_barrier((stats, place))
    far_probs = pltpu.VMEM((2, rows, 2 * rows), BF)
    far_rows = pltpu.VMEM((2, 2 * rows, pair), BF)
    final, d_ef, d_of, dq_far = call(
        far_kernel, (stat_shape, kv_shape, kv_shape, part_shape), (pairs,),
        [win] * 2 + [near, bias_spec, stat_spec], (stat_spec, win, win, part_spec),
        scratch=(far_probs, far_probs, far_rows, far_rows), estimate=cost(8 * step, 2 << 20),
    )(ids, ef, of, qg, bias, stats)
    back_ef = chip_swapped(d_ef, 0)
    back_of = chip_swapped(d_of, 1)
    d_ea, d_oa, d_eb, d_ob, dq_near = call(
        near_kernel, (kv_shape,) * 4 + (part_shape,), (pairs,), [win] * 4 + [near, bias_spec, stat_spec, part_spec],
        (win,) * 4 + (part_spec,), scratch=scratch(4), estimate=cost(32 * step, 4 << 20),
    )(ids, ea, oa, eb, ob, qg, bias, final, dq_far)
    back_eb = chip_swapped(d_eb, 0)
    back_ob = chip_swapped(d_ob, 1)
    back_ea = chip_swapped(joined(d_ea, back_of), 0)
    back_oa = chip_swapped(joined(d_oa, back_ef), 1)
    own_shape = sds((2, rows, half), F32)
    d_a, d_b, dq_own, dq_send = call(
        local_kernel, (own_shape, own_shape, sds((rows, half), BF), sds((rows, half), BF)), (pairs,),
        [win] * 2 + [near, bias_spec, stat_spec, part_spec], (win, win, dq_spec, dq_spec),
        scratch=scratch(2), estimate=cost(16 * step, 4 << 20),
    )(ids, a, b, qg, bias, final, dq_near)
    dq_got = core_swapped(dq_send)
    q_other, q_own = call(
        query_kernel, (sds((rows, cols), F32), sds((rows, cols), F32)), (1,),
        [whole(rows, half)] * 2 + [whole(2 * cols, cols)], (whole(rows, cols), whole(rows, cols)),
        estimate=cost(2 * rows * cols * 2 * cols, 3 << 20),
    )(ids, dq_own, dq_got, q_weight)
    d_a, q_other, q_own = lax.optimization_barrier((d_a, q_other, q_own))
    keep, give = call(
        total_kernel, (kv_shape, kv_shape), (1,), [kv_whole] * 6, (kv_whole, kv_whole),
    )(ids, d_a, d_b, back_ea, back_oa, back_eb, back_ob)
    gave = core_swapped(give)
    weight_keep = pl.BlockSpec((cols, half), lambda i, p: (1 - p[2], p[0]))
    weight_gave = pl.BlockSpec((cols, half), lambda i, p: (1 - p[2], 1 - p[0]))
    weight_own = pl.BlockSpec((cols, cols), lambda i, p: (p[2], 0))
    add_cost = cost(2 * rows * cols * 2 * half, 2 << 20)
    partial_keep = call(
        add_kernel, sds((rows, cols), F32), (1,), [whole(rows, cols), kv_whole] + [weight_keep] * 2,
        whole(rows, cols), estimate=add_cost,
    )(ids, q_other, keep, k_weight, v_weight)
    partial_other = call(
        add_kernel, sds((rows, cols), BF), (1,), [whole(rows, cols), kv_whole] + [weight_gave] * 2,
        whole(rows, cols), estimate=add_cost,
    )(ids, partial_keep, gave, k_weight, v_weight)
    partial_got = lax.ppermute(partial_other, "head", [(0, 1), (1, 0)])
    partial_own = call(
        both_kernel, sds((rows, cols), F32), (1,),
        [whole(rows, cols)] + [kv_whole] * 2 + [weight_own] * 2, whole(rows, cols),
        estimate=cost(2 * rows * cols * 2 * cols, 2 << 20),
    )(ids, q_own, keep, gave, k_weight, v_weight)
    outgoing = call(
        scatter_kernel, sds((slots, cols), BF), (1,),
        [whole(rows, cols), whole(rows, cols), whole(slots, rows)], whole(slots, cols), scalars=0,
        estimate=cost(2 * slots * rows * cols, 2 << 20),
    )(partial_own, partial_got, place)
    arrived = lax.all_to_all(
        outgoing, "blk", split_axis=0, concat_axis=0, tiled=True, axis_index_groups=[order]
    )
    home = [int(g) for g in np.argsort(np.array(order[::4]) // 4)]
    return call(
        functools.partial(restore_kernel, home=home), sds((slots, cols), BF), (1,), [whole(slots, cols)],
        whole(slots, cols), scalars=0,
    )(arrived)


def solution(mesh):
    return jax.shard_map(
        on_device,
        mesh=mesh,
        in_specs=(
            P("blk", "head"),
            P("blk", "head"),
            P("blk", "head"),
            P("blk", "head"),
            P(None, "head"),
            P(None, "head"),
            P(None, "head"),
            P("blk", None),
            P("blk", None),
        ),
        out_specs=P("blk", "head"),
        check_vma=False,
    )
```

```python
import functools
import math

import jax
import jax.numpy as jnp
import numpy as np
from jax import lax
from jax.experimental import pallas as pl
from jax.experimental.pallas import tpu as pltpu
from jax.sharding import PartitionSpec as P

HD = 64
BLOCK = 128
REACH = 3
SPAN = 2 * REACH + 1
LOG2E = math.log2(math.e)
MASKED = -1e30
FLOOR = -1e29
CAP = 4
BF = jnp.bfloat16
F32 = jnp.float32
NT = (((1,), (1,)), ((), ()))
NN = (((1,), (0,)), ((), ()))
TN = (((0,), (0,)), ((), ()))


def dot(a, b, dims):
    return lax.dot_general(a, b, dims, preferred_element_type=F32)


def core_swapped(value):
    count = lax.axis_size("blk")
    return lax.ppermute(value, "blk", [(s, s ^ 1) for s in range(count)])


def chip_swapped(value, odd):
    count = lax.axis_size("blk")
    ahead = [2 if (s // 2) % 2 == odd else -2 for s in range(count)]
    return lax.ppermute(value, "blk", [(s, (s + ahead[s]) % count) for s in range(count)])


def bias_rows(adj_ref):
    shape = (16, 2 * BLOCK)
    row = lax.broadcasted_iota(jnp.int32, shape, 0)
    query_block = lax.broadcasted_iota(jnp.int32, shape, 1) // BLOCK
    allowed = row == 2 * REACH + query_block
    for c in range(2 * SPAN):
        for b in range(2):
            hit = (row == c) & (query_block == b) & (adj_ref[b, c] > 0)
            allowed = allowed | hit
    return jnp.where(allowed, 0.0, MASKED)


def with_place(kernel, core_ref, chip_ref, head_ref, *refs):
    kernel((core_ref[0], chip_ref[0], head_ref[0]), *refs)


def pack_kernel(ids, adj_in_ref, k_ref, v_ref, q_ref, g_ref, send_ref, own_ref, adj_ref, sems):
    rows, cols = k_ref.shape
    half = cols // 2
    copies = [pltpu.make_async_copy(adj_in_ref, adj_ref, sems.at[0])]
    for to_ref, which in ((send_ref, 1 - ids[0]), (own_ref, ids[0])):
        at = pl.ds(pl.multiple_of(which * half, half), half)
        for n, from_ref in enumerate((k_ref, v_ref, q_ref, g_ref)):
            copies.append(
                pltpu.make_async_copy(
                    from_ref.at[:, at], to_ref.at[0:rows, n * half : (n + 1) * half], sems.at[len(copies)]
                )
            )
    for copy in copies:
        copy.start()
    copies[0].wait()
    bias = bias_rows(adj_ref).astype(BF)
    for to_ref in (send_ref, own_ref):
        to_ref[rows : rows + 16, 0:half] = bias
        to_ref[rows : rows + 16, half:] = jnp.zeros((16, 3 * half), BF)
    for copy in copies[1:]:
        copy.wait()


def order_kernel(ids, own_ref, got_ref, a_ref, b_ref, qg_ref, bias_ref):
    rows = a_ref.shape[1]
    cols = a_ref.shape[2]
    par = ids[0]
    scale = 1.0 / math.sqrt(HD)
    for sector, from_ref in ((par, own_ref), (1 - par, got_ref)):
        qg_ref[0, sector] = from_ref[0:rows, 2 * cols : 3 * cols] * scale
        qg_ref[1, sector] = from_ref[0:rows, 3 * cols : 4 * cols]
        bias_ref[sector] = from_ref[rows : rows + 16, 0:cols].astype(F32)
    b_own = par == ids[1]
    for which in range(2):
        own = own_ref[0:rows, which * cols : (which + 1) * cols]
        got = got_ref[0:rows, which * cols : (which + 1) * cols]
        a_ref[which] = jnp.where(b_own, got, own)
        b_ref[which] = jnp.where(b_own, own, got)


def one_head(pair_ref, h):
    value = pair_ref[...]
    lane_head = lax.broadcasted_iota(jnp.int32, value.shape, 1) // HD
    return jnp.where(lane_head == h, value, 0.0).astype(BF)


def bias_pair_of(bias_ref, t, j):
    return [bias_ref[t, pl.ds(2 * j + b, 1), :] for b in range(2)]


def fold_stats(stats, key_value, query_head, grad_head, bias_pair):
    scores = dot(key_value[0], query_head, NT)
    grads = dot(key_value[1], grad_head, NT)
    top, total, delta = stats
    for b in range(2):
        at = slice(b * BLOCK, (b + 1) * BLOCK)
        new_top = jnp.maximum(top, jnp.max(scores[at], axis=0, keepdims=True) + bias_pair[b])
        weight = jnp.exp2(scores[at] * LOG2E + (bias_pair[b] - new_top) * LOG2E)
        shrink = jnp.exp2((top - new_top) * LOG2E)
        total = jnp.sum(weight, axis=0, keepdims=True) + total * shrink
        delta = jnp.sum(weight * grads[at], axis=0, keepdims=True) + delta * shrink
        top = new_top
    return (top, total, delta), scores, grads


def fold_windows(names, windows, qg_ref, bias_ref, before_ref, stats_ref):
    rows = qg_ref.shape[2]
    for t in range(2):
        for h in range(2):
            qh = one_head(qg_ref.at[0, t], h)
            gh = one_head(qg_ref.at[1, t], h)
            if before_ref is None:
                zero = jnp.zeros((1, rows), F32)
                stats = (zero + FLOOR, zero, zero)
            else:
                stats = tuple(before_ref[t, h, row : row + 1, :] for row in range(3))
            for w, window in zip(names, windows):
                stats, _, _ = fold_stats(stats, window, qh, gh, bias_pair_of(bias_ref, t, w - t))
            for row in range(3):
                stats_ref[t, h, row : row + 1, :] = stats[row]


def first_stats_kernel(ids, a_ref, b_ref, ea_ref, eb_ref, qg_ref, bias_ref, stats_ref):
    odd = ids[1]
    names = (4 - odd, 3 + odd, 5 - 3 * odd, 6 - 5 * odd)
    fold_windows(names, (a_ref, b_ref, ea_ref, eb_ref), qg_ref, bias_ref, None, stats_ref)


def second_stats_kernel(ids, oa_ref, ob_ref, qg_ref, bias_ref, before_ref, stats_ref):
    odd = ids[1]
    names = (2 + 3 * odd, 1 + 5 * odd)
    fold_windows(names, (oa_ref, ob_ref), qg_ref, bias_ref, before_ref, stats_ref)


def head_rows_of(first, second):
    row_head = lax.broadcasted_iota(jnp.int32, first.shape, 0) // HD
    return jnp.where(row_head == 0, first, second)


def query_grad(keys_t, grads, rows):
    both = dot(keys_t, grads, NN)
    return head_rows_of(both[:, 0:rows], both[:, rows:])


def flipped(value):
    return jnp.transpose(value.astype(F32)).astype(BF)


def far_kernel(
    ids, e_ref, o_ref, qg_ref, bias_ref, stats_ref, final_ref, de_ref, do_ref, dq_ref,
    ps_ref, ds_ref, qs_ref, gs_ref,
):
    rows = qg_ref.shape[2]
    odd = ids[1]
    for n, (t, window, out_ref) in enumerate(((1 - odd, e_ref, de_ref), (odd, o_ref, do_ref))):
        for h in range(2):
            cols = slice(h * rows, (h + 1) * rows)
            qh = one_head(qg_ref.at[0, t], h)
            gh = one_head(qg_ref.at[1, t], h)
            qs_ref[n, cols, :] = qh
            gs_ref[n, cols, :] = gh
            bias_pair = bias_pair_of(bias_ref, t, (SPAN - 1) * t)
            stats = tuple(stats_ref[t, h, row : row + 1, :] for row in range(3))
            (top, total, delta), scores, grads = fold_stats(stats, window, qh, gh, bias_pair)
            log_total = top * LOG2E + jnp.log2(total)
            delta = delta / total
            final_ref[t, h, 0:1, :] = log_total
            final_ref[t, h, 1:2, :] = delta
            for b in range(2):
                at = slice(b * BLOCK, (b + 1) * BLOCK)
                prob = jnp.exp2(scores[at] * LOG2E + (bias_pair[b] * LOG2E - log_total))
                ps_ref[n, at, cols] = prob.astype(BF)
                ds_ref[n, at, cols] = (prob * (grads[at] - delta)).astype(BF)
        out_ref[0] = dot(ds_ref[n], qs_ref[n], NN).astype(BF)
        out_ref[1] = dot(ps_ref[n], gs_ref[n], NN).astype(BF)
        dq_ref[0, t] = query_grad(flipped(window[0]), ds_ref[n], rows)


def shared_kernel(names, qg_ref, bias_ref, final_ref, windows, outs, ps_ref, ds_ref, qs_ref, gs_ref, kt_ref):
    rows = qg_ref.shape[2]
    for t in range(2):
        for h in range(2):
            block = 2 * t + h
            cols = slice(block * rows, (block + 1) * rows)
            qs_ref[cols, :] = one_head(qg_ref.at[0, t], h)
            gs_ref[cols, :] = one_head(qg_ref.at[1, t], h)
    for n, (w, window) in enumerate(zip(names, windows)):
        keys = slice(n * rows, (n + 1) * rows)
        kt_ref[:, keys] = flipped(window[0])
        for t in range(2):
            for h in range(2):
                block = 2 * t + h
                cols = slice(block * rows, (block + 1) * rows)
                scores = dot(window[0], qs_ref[cols, :], NT)
                grads = dot(window[1], gs_ref[cols, :], NT)
                log_total = final_ref[t, h, 0:1, :]
                delta = final_ref[t, h, 1:2, :]
                bias_pair = bias_pair_of(bias_ref, t, w - t)
                for b in range(2):
                    at = slice(b * BLOCK, (b + 1) * BLOCK)
                    to = slice(n * rows + b * BLOCK, n * rows + (b + 1) * BLOCK)
                    prob = jnp.exp2(scores[at] * LOG2E + (bias_pair[b] * LOG2E - log_total))
                    ps_ref[to, cols] = prob.astype(BF)
                    ds_ref[to, cols] = (prob * (grads[at] - delta)).astype(BF)
        out_ref = outs[n]
        out_ref[0] = dot(ds_ref[keys, :], qs_ref[...], NN).astype(out_ref.dtype)
        out_ref[1] = dot(ps_ref[keys, :], gs_ref[...], NN).astype(out_ref.dtype)
    return [
        query_grad(kt_ref[...], ds_ref[:, 2 * t * rows : 2 * (t + 1) * rows], rows) for t in range(2)
    ]


def near_kernel(ids, ea_ref, oa_ref, eb_ref, ob_ref, qg_ref, bias_ref, final_ref, part_ref, *refs):
    outs, dq_ref, scratch = refs[0:4], refs[4], refs[5:]
    odd = ids[1]
    names = (5 - 3 * odd, 2 + 3 * odd, 6 - 5 * odd, 1 + 5 * odd)
    grads = shared_kernel(names, qg_ref, bias_ref, final_ref, (ea_ref, oa_ref, eb_ref, ob_ref), outs, *scratch)
    for t in range(2):
        dq_ref[0, t] = part_ref[0, t] + grads[t]


def local_kernel(ids, a_ref, b_ref, qg_ref, bias_ref, final_ref, part_ref, *refs):
    outs, (dq_own_ref, dq_send_ref), scratch = refs[0:2], refs[2:4], refs[4:]
    odd = ids[1]
    grads = shared_kernel((4 - odd, 3 + odd), qg_ref, bias_ref, final_ref, (a_ref, b_ref), outs, *scratch)
    total = [part_ref[0, t] + grads[t] for t in range(2)]
    first = ids[0] == 0
    scale = 1.0 / math.sqrt(HD)
    dq_own_ref[...] = jnp.transpose(jnp.where(first, total[0], total[1]) * scale).astype(BF)
    dq_send_ref[...] = jnp.transpose(jnp.where(first, total[1], total[0]) * scale).astype(BF)


def joined(first, second):
    return (first.astype(F32) + second.astype(F32)).astype(BF)


def total_kernel(ids, a_ref, b_ref, ea_ref, oa_ref, eb_ref, ob_ref, keep_ref, send_ref):
    b_own = ids[0] == ids[1]
    for which in range(2):
        value_a = a_ref[which] + ob_ref[which].astype(F32) + ea_ref[which].astype(F32)
        value_b = b_ref[which] + eb_ref[which].astype(F32) + oa_ref[which].astype(F32)
        keep_ref[which] = jnp.where(b_own, value_b, value_a).astype(BF)
        send_ref[which] = jnp.where(b_own, value_a, value_b).astype(BF)


def query_kernel(ids, own_ref, got_ref, weight_ref, other_out_ref, own_out_ref):
    first = ids[0] == 0
    half = own_ref.shape[1]
    low = jnp.where(first, own_ref[...], got_ref[...])
    high = jnp.where(first, got_ref[...], own_ref[...])
    cols = own_out_ref.shape[1]
    here = ids[2]
    for out_ref, which in ((other_out_ref, 1 - here), (own_out_ref, here)):
        at = pl.ds(pl.multiple_of(which * cols, cols), cols)
        out_ref[...] = dot(low, weight_ref[at, 0:half], NT) + dot(high, weight_ref[at, half:], NT)


def add_kernel(ids, base_ref, grads_ref, wk_ref, wv_ref, out_ref):
    value = base_ref[...] + dot(grads_ref[0], wk_ref[...], NT) + dot(grads_ref[1], wv_ref[...], NT)
    out_ref[...] = value.astype(out_ref.dtype)


def both_kernel(ids, base_ref, keep_ref, gave_ref, wk_ref, wv_ref, out_ref):
    first = ids[0] == 0
    half = keep_ref.shape[2]
    value = base_ref[...]
    for which, weight in ((0, wk_ref), (1, wv_ref)):
        low = jnp.where(first, keep_ref[which], gave_ref[which])
        high = jnp.where(first, gave_ref[which], keep_ref[which])
        value = value + dot(low, weight[:, 0:half], NT) + dot(high, weight[:, half:], NT)
    out_ref[...] = value


def route_kernel(owner_col_ref, owner_row_ref, label_ref, place_ref):
    rows = owner_col_ref.shape[0]
    owner_row = owner_row_ref[...]
    earlier = lax.broadcasted_iota(jnp.int32, (rows, rows), 0) < lax.broadcasted_iota(jnp.int32, (rows, rows), 1)
    same = (owner_col_ref[...] == owner_row) & earlier
    rank = jnp.sum(same.astype(jnp.int32), axis=0, keepdims=True)
    target = owner_row * CAP + rank
    place_ref[...] = jnp.where(label_ref[...] == target, 1.0, 0.0).astype(BF)


def scatter_kernel(own_ref, got_ref, place_ref, out_ref):
    value = (own_ref[...] + got_ref[...].astype(F32)).astype(BF)
    out_ref[...] = dot(place_ref[...], value, NN).astype(BF)


def spread_order(count):
    groups = [int(g) for g in np.random.default_rng(1).permutation(count // 4)]
    return [4 * g + i for g in groups for i in range(4)]


def restore_kernel(from_ref, out_ref, *, home):
    rows = out_ref.shape[0] // len(home)
    for i, g in enumerate(home):
        out_ref[i * rows : (i + 1) * rows, :] = from_ref[g * rows : (g + 1) * rows, :]


def cost(flops, moved_bytes, exps=0):
    return pl.CostEstimate(flops=flops, bytes_accessed=moved_bytes, transcendentals=exps)


def on_device(query, key, value, out_grad, q_weight, k_weight, v_weight, adjacency, owner):
    rows, cols = query.shape
    half = cols // 2
    pair = 2 * HD
    sds = jax.ShapeDtypeStruct
    block = lax.axis_index("blk")
    ids = tuple(
        jnp.reshape(value, (1,)).astype(jnp.int32)
        for value in (block & 1, (block >> 1) & 1, lax.axis_index("head"))
    )
    smem = pl.BlockSpec(memory_space=pltpu.SMEM)
    hbm = pl.BlockSpec(memory_space=pltpu.HBM)

    def call(kernel, outs, grid, in_specs, out_specs, scratch=(), placed=True, estimate=None, limit=16):
        return pl.pallas_call(
            functools.partial(with_place, kernel) if placed else kernel,
            out_shape=outs,
            grid_spec=pltpu.PrefetchScalarGridSpec(
                num_scalar_prefetch=3 if placed else 0, grid=grid, in_specs=in_specs, out_specs=out_specs,
                scratch_shapes=list(scratch),
            ),
            compiler_params=pltpu.CompilerParams(vmem_limit_bytes=limit << 20),
            cost_estimate=estimate,
        )

    def whole(*shape):
        return pl.BlockSpec(shape, lambda i, *p: (0,) * len(shape))

    packed = sds((rows + 16, 4 * half), BF)
    send, own = call(
        pack_kernel, (packed, packed), (1,), [hbm] * 5, (whole(rows + 16, 4 * half),) * 2,
        scratch=(pltpu.SMEM(adjacency.shape, jnp.int32), pltpu.SemaphoreType.DMA((9,))),
    )(*ids, *[pltpu.with_memory_space_constraint(x, pltpu.HBM) for x in (adjacency, key, value, query, out_grad)])
    got = core_swapped(send)
    kv_shape = sds((2, rows, half), BF)
    kv_whole = whole(2, rows, half)
    a, b, qg, bias = call(
        order_kernel,
        (kv_shape, kv_shape, sds((2, 2, rows, half), BF), sds((2, 16, rows), F32)),
        (1,),
        [whole(rows + 16, 4 * half)] * 2,
        (kv_whole, kv_whole, whole(2, 2, rows, half), whole(2, 16, rows)),
    )(*ids, own, got)
    ea = chip_swapped(a, 0)
    oa = chip_swapped(b, 1)
    eb = chip_swapped(b, 0)
    ob = chip_swapped(a, 1)
    ef = chip_swapped(oa, 0)
    of = chip_swapped(ea, 1)

    count = lax.axis_size("blk")
    slots = CAP * count
    order = spread_order(count)
    labels = jnp.asarray(np.array([[CAP * s + r] for s in order for r in range(CAP)], np.int32))
    place = call(
        route_kernel, sds((slots, rows), BF), (1,),
        [whole(rows, 1), whole(1, rows), whole(slots, 1)], whole(slots, rows), placed=False,
        estimate=cost(rows * rows * 8, 1 << 20),
    )(owner, owner.reshape(1, rows), labels)

    pairs = half // pair
    win = pl.BlockSpec((2, rows, pair), lambda i, *p: (0, 0, i))
    near = pl.BlockSpec((2, 2, rows, pair), lambda i, *p: (0, 0, 0, i))
    dq_spec = pl.BlockSpec((rows, pair), lambda i, *p: (0, i))
    stat_spec = pl.BlockSpec((2, 2, 8, rows), lambda i, *p: (0, i, 0, 0))
    bias_spec = whole(2, 16, rows)
    stat_shape = sds((2, 2 * pairs, 8, rows), F32)
    step = 2 * rows * rows * HD * 4
    part_shape = sds((pairs, 2, pair, rows), F32)
    part_spec = pl.BlockSpec((1, 2, pair, rows), lambda i, *p: (i, 0, 0, 0))

    def scratch(blocks):
        return (
            pltpu.VMEM((blocks * rows, 4 * rows), BF),
            pltpu.VMEM((blocks * rows, 4 * rows), BF),
            pltpu.VMEM((4 * rows, pair), BF),
            pltpu.VMEM((4 * rows, pair), BF),
            pltpu.VMEM((pair, blocks * rows), BF),
        )

    stats = call(
        first_stats_kernel, stat_shape, (pairs,), [win] * 4 + [near, bias_spec], stat_spec,
        estimate=cost(16 * step, 4 << 20),
    )(*ids, a, b, ea, eb, qg, bias)
    stats = call(
        second_stats_kernel, stat_shape, (pairs,), [win] * 2 + [near, bias_spec, stat_spec], stat_spec,
        estimate=cost(8 * step, 2 << 20),
    )(*ids, oa, ob, qg, bias, stats)
    stats, place = lax.optimization_barrier((stats, place))
    far_probs = pltpu.VMEM((2, rows, 2 * rows), BF)
    far_rows = pltpu.VMEM((2, 2 * rows, pair), BF)
    final, d_ef, d_of, dq_far = call(
        far_kernel, (stat_shape, kv_shape, kv_shape, part_shape), (pairs,),
        [win] * 2 + [near, bias_spec, stat_spec], (stat_spec, win, win, part_spec),
        scratch=(far_probs, far_probs, far_rows, far_rows), estimate=cost(8 * step, 2 << 20),
    )(*ids, ef, of, qg, bias, stats)
    back_ef = chip_swapped(d_ef, 0)
    back_of = chip_swapped(d_of, 1)
    d_ea, d_oa, d_eb, d_ob, dq_near = call(
        near_kernel, (kv_shape,) * 4 + (part_shape,), (pairs,), [win] * 4 + [near, bias_spec, stat_spec, part_spec],
        (win,) * 4 + (part_spec,), scratch=scratch(4), estimate=cost(32 * step, 4 << 20),
    )(*ids, ea, oa, eb, ob, qg, bias, final, dq_far)
    back_eb = chip_swapped(d_eb, 0)
    back_ob = chip_swapped(d_ob, 1)
    back_ea = chip_swapped(joined(d_ea, back_of), 0)
    back_oa = chip_swapped(joined(d_oa, back_ef), 1)
    own_shape = sds((2, rows, half), F32)
    d_a, d_b, dq_own, dq_send = call(
        local_kernel, (own_shape, own_shape, sds((rows, half), BF), sds((rows, half), BF)), (pairs,),
        [win] * 2 + [near, bias_spec, stat_spec, part_spec], (win, win, dq_spec, dq_spec),
        scratch=scratch(2), estimate=cost(16 * step, 4 << 20),
    )(*ids, a, b, qg, bias, final, dq_near)
    dq_got = core_swapped(dq_send)
    q_other, q_own = call(
        query_kernel, (sds((rows, cols), F32), sds((rows, cols), F32)), (1,),
        [whole(rows, half)] * 2 + [whole(2 * cols, cols)], (whole(rows, cols), whole(rows, cols)),
        estimate=cost(2 * rows * cols * 2 * cols, 3 << 20),
    )(*ids, dq_own, dq_got, q_weight)
    d_a, q_other, q_own = lax.optimization_barrier((d_a, q_other, q_own))
    keep, give = call(
        total_kernel, (kv_shape, kv_shape), (1,), [kv_whole] * 6, (kv_whole, kv_whole),
    )(*ids, d_a, d_b, back_ea, back_oa, back_eb, back_ob)
    gave = core_swapped(give)
    weight_keep = pl.BlockSpec((cols, half), lambda i, *p: (1 - p[2][0], p[0][0]))
    weight_gave = pl.BlockSpec((cols, half), lambda i, *p: (1 - p[2][0], 1 - p[0][0]))
    weight_own = pl.BlockSpec((cols, cols), lambda i, *p: (p[2][0], 0))
    add_cost = cost(2 * rows * cols * 2 * half, 2 << 20)
    partial_keep = call(
        add_kernel, sds((rows, cols), F32), (1,), [whole(rows, cols), kv_whole] + [weight_keep] * 2,
        whole(rows, cols), estimate=add_cost,
    )(*ids, q_other, keep, k_weight, v_weight)
    partial_other = call(
        add_kernel, sds((rows, cols), BF), (1,), [whole(rows, cols), kv_whole] + [weight_gave] * 2,
        whole(rows, cols), estimate=add_cost,
    )(*ids, partial_keep, gave, k_weight, v_weight)
    partial_got = lax.ppermute(partial_other, "head", [(0, 1), (1, 0)])
    partial_own = call(
        both_kernel, sds((rows, cols), F32), (1,),
        [whole(rows, cols)] + [kv_whole] * 2 + [weight_own] * 2, whole(rows, cols),
        estimate=cost(2 * rows * cols * 2 * cols, 2 << 20),
    )(*ids, q_own, keep, gave, k_weight, v_weight)
    outgoing = call(
        scatter_kernel, sds((slots, cols), BF), (1,),
        [whole(rows, cols), whole(rows, cols), whole(slots, rows)], whole(slots, cols), placed=False,
        estimate=cost(2 * slots * rows * cols, 2 << 20),
    )(partial_own, partial_got, place)
    arrived = lax.all_to_all(
        outgoing, "blk", split_axis=0, concat_axis=0, tiled=True, axis_index_groups=[order]
    )
    home = [int(g) for g in np.argsort(np.array(order[::4]) // 4)]
    return call(
        functools.partial(restore_kernel, home=home), sds((slots, cols), BF), (1,), [whole(slots, cols)],
        whole(slots, cols), placed=False,
    )(arrived)


def solution(mesh):
    return jax.shard_map(
        on_device,
        mesh=mesh,
        in_specs=(
            P("blk", "head"),
            P("blk", "head"),
            P("blk", "head"),
            P("blk", "head"),
            P(None, "head"),
            P(None, "head"),
            P(None, "head"),
            P("blk", None),
            P("blk", None),
        ),
        out_specs=P("blk", "head"),
        check_vma=False,
    )
```

```python
import functools
import math

import jax
import jax.numpy as jnp
import numpy as np
from jax import lax
from jax.experimental import pallas as pl
from jax.experimental.pallas import tpu as pltpu
from jax.sharding import PartitionSpec as P

HD = 64
BLOCK = 128
REACH = 3
SPAN = 2 * REACH + 1
LOG2E = math.log2(math.e)
MASKED = -1e30
FLOOR = -1e29
CAP = 4
BF = jnp.bfloat16
F32 = jnp.float32
NT = (((1,), (1,)), ((), ()))
NN = (((1,), (0,)), ((), ()))
TN = (((0,), (0,)), ((), ()))


def dot(a, b, dims):
    return lax.dot_general(a, b, dims, preferred_element_type=F32)


def core_swapped(value):
    count = lax.axis_size("blk")
    return lax.ppermute(value, "blk", [(s, s ^ 1) for s in range(count)])


def chip_swapped(value, odd):
    count = lax.axis_size("blk")
    ahead = [-2 if (s // 2) % 2 == odd else 2 for s in range(count)]
    return lax.ppermute(value, "blk", [(s, (s + ahead[s]) % count) for s in range(count)])


def bias_rows(adj_ref):
    shape = (16, 2 * BLOCK)
    row = lax.broadcasted_iota(jnp.int32, shape, 0)
    query_block = lax.broadcasted_iota(jnp.int32, shape, 1) // BLOCK
    allowed = row == 2 * REACH + query_block
    for c in range(2 * SPAN):
        for b in range(2):
            hit = (row == c) & (query_block == b) & (adj_ref[b, c] > 0)
            allowed = allowed | hit
    return jnp.where(allowed, 0.0, MASKED)


def with_place(kernel, core_ref, chip_ref, head_ref, *refs):
    kernel((core_ref[0], chip_ref[0], head_ref[0]), *refs)


def pack_kernel(ids, adj_in_ref, k_ref, v_ref, q_ref, g_ref, send_ref, own_ref, adj_ref, sems):
    rows, cols = k_ref.shape
    half = cols // 2
    copies = [pltpu.make_async_copy(adj_in_ref, adj_ref, sems.at[0])]
    for to_ref, which in ((send_ref, 1 - ids[0]), (own_ref, ids[0])):
        at = pl.ds(pl.multiple_of(which * half, half), half)
        for n, from_ref in enumerate((k_ref, v_ref, q_ref, g_ref)):
            copies.append(
                pltpu.make_async_copy(
                    from_ref.at[:, at], to_ref.at[0:rows, n * half : (n + 1) * half], sems.at[len(copies)]
                )
            )
    for copy in copies:
        copy.start()
    copies[0].wait()
    bias = bias_rows(adj_ref).astype(BF)
    for to_ref in (send_ref, own_ref):
        to_ref[rows : rows + 16, 0:half] = bias
        to_ref[rows : rows + 16, half:] = jnp.zeros((16, 3 * half), BF)
    for copy in copies[1:]:
        copy.wait()


def order_kernel(ids, own_ref, got_ref, a_ref, b_ref, qg_ref, bias_ref):
    rows = a_ref.shape[1]
    cols = a_ref.shape[2]
    par = ids[0]
    scale = 1.0 / math.sqrt(HD)
    for sector, from_ref in ((par, own_ref), (1 - par, got_ref)):
        qg_ref[0, sector] = from_ref[0:rows, 2 * cols : 3 * cols] * scale
        qg_ref[1, sector] = from_ref[0:rows, 3 * cols : 4 * cols]
        bias_ref[sector] = from_ref[rows : rows + 16, 0:cols].astype(F32)
    b_own = par == ids[1]
    for which in range(2):
        own = own_ref[0:rows, which * cols : (which + 1) * cols]
        got = got_ref[0:rows, which * cols : (which + 1) * cols]
        a_ref[which] = jnp.where(b_own, got, own)
        b_ref[which] = jnp.where(b_own, own, got)


def one_head(pair_ref, h):
    value = pair_ref[...]
    lane_head = lax.broadcasted_iota(jnp.int32, value.shape, 1) // HD
    return jnp.where(lane_head == h, value, 0.0).astype(BF)


def bias_pair_of(bias_ref, t, j):
    return [bias_ref[t, pl.ds(2 * j + b, 1), :] for b in range(2)]


def fold_stats(stats, key_value, query_head, grad_head, bias_pair):
    scores = dot(key_value[0], query_head, NT)
    grads = dot(key_value[1], grad_head, NT)
    top, total, delta = stats
    for b in range(2):
        at = slice(b * BLOCK, (b + 1) * BLOCK)
        new_top = jnp.maximum(top, jnp.max(scores[at], axis=0, keepdims=True) + bias_pair[b])
        weight = jnp.exp2(scores[at] * LOG2E + (bias_pair[b] - new_top) * LOG2E)
        shrink = jnp.exp2((top - new_top) * LOG2E)
        total = jnp.sum(weight, axis=0, keepdims=True) + total * shrink
        delta = jnp.sum(weight * grads[at], axis=0, keepdims=True) + delta * shrink
        top = new_top
    return (top, total, delta), scores, grads


def fold_windows(names, windows, qg_ref, bias_ref, before_ref, stats_ref):
    rows = qg_ref.shape[2]
    for t in range(2):
        for h in range(2):
            qh = one_head(qg_ref.at[0, t], h)
            gh = one_head(qg_ref.at[1, t], h)
            if before_ref is None:
                zero = jnp.zeros((1, rows), F32)
                stats = (zero + FLOOR, zero, zero)
            else:
                stats = tuple(before_ref[t, h, row : row + 1, :] for row in range(3))
            for w, window in zip(names, windows):
                stats, _, _ = fold_stats(stats, window, qh, gh, bias_pair_of(bias_ref, t, w - t))
            for row in range(3):
                stats_ref[t, h, row : row + 1, :] = stats[row]


def first_stats_kernel(ids, a_ref, b_ref, oa_ref, ob_ref, qg_ref, bias_ref, stats_ref):
    odd = ids[1]
    names = (4 - odd, 3 + odd, 2 + 3 * odd, 1 + 5 * odd)
    fold_windows(names, (a_ref, b_ref, oa_ref, ob_ref), qg_ref, bias_ref, None, stats_ref)


def second_stats_kernel(ids, ea_ref, eb_ref, qg_ref, bias_ref, before_ref, stats_ref):
    odd = ids[1]
    names = (5 - 3 * odd, 6 - 5 * odd)
    fold_windows(names, (ea_ref, eb_ref), qg_ref, bias_ref, before_ref, stats_ref)


def head_rows_of(first, second):
    row_head = lax.broadcasted_iota(jnp.int32, first.shape, 0) // HD
    return jnp.where(row_head == 0, first, second)


def query_grad(keys_t, grads, rows):
    both = dot(keys_t, grads, NN)
    return head_rows_of(both[:, 0:rows], both[:, rows:])


def flipped(value):
    return jnp.transpose(value.astype(F32)).astype(BF)


def far_kernel(
    ids, e_ref, o_ref, qg_ref, bias_ref, stats_ref, final_ref, de_ref, do_ref, ds_ref, ps_ref, qs_ref, gs_ref
):
    rows = qg_ref.shape[2]
    odd = ids[1]
    sides = ((1 - odd, e_ref, de_ref), (odd, o_ref, do_ref))
    halves = [slice(b * BLOCK, (b + 1) * BLOCK) for b in range(2)]
    items = [(n, h) for n in range(2) for h in range(2)]
    scores, grads, biases = [], [], []
    for n, h in items:
        t, window, _ = sides[n]
        cols = slice(h * rows, (h + 1) * rows)
        qh = one_head(qg_ref.at[0, t], h)
        gh = one_head(qg_ref.at[1, t], h)
        qs_ref[n, cols, :] = qh
        gs_ref[n, cols, :] = gh
        scores.append(dot(window[0], qh, NT))
        grads.append(dot(window[1], gh, NT))
        biases.append(bias_pair_of(bias_ref, t, (SPAN - 1) * t))
    before = [[stats_ref[sides[n][0], h, row : row + 1, :] for row in range(3)] for n, h in items]
    tops = []
    for value, bias, (top, _, _) in zip(scores, biases, before):
        for at, block_bias in zip(halves, bias):
            top = jnp.maximum(top, jnp.max(value[at], axis=0, keepdims=True) + block_bias)
        tops.append(top)
    weights, totals, deltas = [], [], []
    for value, grad, bias, top, (old, total, delta) in zip(scores, grads, biases, tops, before):
        shrink = jnp.exp2((old - top) * LOG2E)
        total = total * shrink
        delta = delta * shrink
        parts = []
        for at, block_bias in zip(halves, bias):
            weight = jnp.exp2(value[at] * LOG2E + (block_bias - top) * LOG2E)
            total = total + jnp.sum(weight, axis=0, keepdims=True)
            delta = delta + jnp.sum(weight * grad[at], axis=0, keepdims=True)
            parts.append(weight)
        weights.append(parts)
        totals.append(total)
        deltas.append(delta)
    for (n, h), parts, grad, top, total, delta in zip(items, weights, grads, tops, totals, deltas):
        cols = slice(h * rows, (h + 1) * rows)
        scale = 1.0 / total
        delta = delta * scale
        final_ref[sides[n][0], h, 0:1, :] = top * LOG2E + jnp.log2(total)
        final_ref[sides[n][0], h, 1:2, :] = delta
        for at, weight in zip(halves, parts):
            prob = weight * scale
            ps_ref[n, at, cols] = prob.astype(BF)
            ds_ref[0, n, at, cols] = (prob * (grad[at] - delta)).astype(BF)
    for n in range(2):
        out_ref = sides[n][2]
        out_ref[0] = dot(ds_ref[0, n], qs_ref[n], NN).astype(BF)
        out_ref[1] = dot(ps_ref[n], gs_ref[n], NN).astype(BF)


def shared_kernel(names, qg_ref, bias_ref, final_ref, windows, outs, ps_ref, ds_ref, qs_ref, gs_ref, kt_ref):
    rows = qg_ref.shape[2]
    for t in range(2):
        for h in range(2):
            block = 2 * t + h
            cols = slice(block * rows, (block + 1) * rows)
            qs_ref[cols, :] = one_head(qg_ref.at[0, t], h)
            gs_ref[cols, :] = one_head(qg_ref.at[1, t], h)
    for n, (w, window) in enumerate(zip(names, windows)):
        keys = slice(n * rows, (n + 1) * rows)
        kt_ref[:, keys] = flipped(window[0])
        for t in range(2):
            for h in range(2):
                block = 2 * t + h
                cols = slice(block * rows, (block + 1) * rows)
                scores = dot(window[0], qs_ref[cols, :], NT)
                grads = dot(window[1], gs_ref[cols, :], NT)
                log_total = final_ref[t, h, 0:1, :]
                delta = final_ref[t, h, 1:2, :]
                bias_pair = bias_pair_of(bias_ref, t, w - t)
                for b in range(2):
                    at = slice(b * BLOCK, (b + 1) * BLOCK)
                    to = slice(n * rows + b * BLOCK, n * rows + (b + 1) * BLOCK)
                    prob = jnp.exp2(scores[at] * LOG2E + (bias_pair[b] * LOG2E - log_total))
                    ps_ref[to, cols] = prob.astype(BF)
                    ds_ref[to, cols] = (prob * (grads[at] - delta)).astype(BF)
        out_ref = outs[n]
        out_ref[0] = dot(ds_ref[keys, :], qs_ref[...], NN).astype(out_ref.dtype)
        out_ref[1] = dot(ps_ref[keys, :], gs_ref[...], NN).astype(out_ref.dtype)
    return [
        query_grad(kt_ref[...], ds_ref[:, 2 * t * rows : 2 * (t + 1) * rows], rows) for t in range(2)
    ]


def near_kernel(ids, ea_ref, oa_ref, eb_ref, ob_ref, qg_ref, bias_ref, final_ref, *refs):
    outs, dq_ref, scratch = refs[0:4], refs[4], refs[5:]
    odd = ids[1]
    names = (5 - 3 * odd, 2 + 3 * odd, 6 - 5 * odd, 1 + 5 * odd)
    grads = shared_kernel(names, qg_ref, bias_ref, final_ref, (ea_ref, oa_ref, eb_ref, ob_ref), outs, *scratch)
    for t in range(2):
        dq_ref[0, t] = grads[t]


def local_kernel(ids, a_ref, b_ref, ef_ref, of_ref, qg_ref, bias_ref, final_ref, part_ref, far_ref, *refs):
    outs, (dq_own_ref, dq_send_ref), scratch = refs[0:2], refs[2:4], refs[4:]
    rows = qg_ref.shape[2]
    odd = ids[1]
    grads = shared_kernel((4 - odd, 3 + odd), qg_ref, bias_ref, final_ref, (a_ref, b_ref), outs, *scratch)
    far_e = query_grad(flipped(ef_ref[0]), far_ref[0, 0], rows)
    far_o = query_grad(flipped(of_ref[0]), far_ref[0, 1], rows)
    even = odd == 0
    far = (jnp.where(even, far_o, far_e), jnp.where(even, far_e, far_o))
    total = [part_ref[0, t] + grads[t] + far[t] for t in range(2)]
    first = ids[0] == 0
    scale = 1.0 / math.sqrt(HD)
    dq_own_ref[...] = jnp.transpose(jnp.where(first, total[0], total[1]) * scale).astype(BF)
    dq_send_ref[...] = jnp.transpose(jnp.where(first, total[1], total[0]) * scale).astype(BF)


def joined(first, second):
    return (first.astype(F32) + second.astype(F32)).astype(BF)


def total_kernel(ids, a_ref, b_ref, ea_ref, oa_ref, eb_ref, ob_ref, keep_ref, send_ref):
    b_own = ids[0] == ids[1]
    for which in range(2):
        value_a = a_ref[which] + ob_ref[which].astype(F32) + ea_ref[which].astype(F32)
        value_b = b_ref[which] + eb_ref[which].astype(F32) + oa_ref[which].astype(F32)
        keep_ref[which] = jnp.where(b_own, value_b, value_a).astype(BF)
        send_ref[which] = jnp.where(b_own, value_a, value_b).astype(BF)


def query_kernel(ids, own_ref, got_ref, weight_ref, other_out_ref, own_out_ref):
    first = ids[0] == 0
    half = own_ref.shape[1]
    low = jnp.where(first, own_ref[...], got_ref[...])
    high = jnp.where(first, got_ref[...], own_ref[...])
    cols = own_out_ref.shape[1]
    here = ids[2]
    for out_ref, which in ((other_out_ref, 1 - here), (own_out_ref, here)):
        at = pl.ds(pl.multiple_of(which * cols, cols), cols)
        out_ref[...] = dot(low, weight_ref[at, 0:half], NT) + dot(high, weight_ref[at, half:], NT)


def add_kernel(ids, base_ref, grads_ref, wk_ref, wv_ref, out_ref):
    value = base_ref[...] + dot(grads_ref[0], wk_ref[...], NT) + dot(grads_ref[1], wv_ref[...], NT)
    out_ref[...] = value.astype(out_ref.dtype)


def both_kernel(ids, base_ref, keep_ref, gave_ref, wk_ref, wv_ref, out_ref):
    first = ids[0] == 0
    half = keep_ref.shape[2]
    value = base_ref[...]
    for which, weight in ((0, wk_ref), (1, wv_ref)):
        low = jnp.where(first, keep_ref[which], gave_ref[which])
        high = jnp.where(first, gave_ref[which], keep_ref[which])
        value = value + dot(low, weight[:, 0:half], NT) + dot(high, weight[:, half:], NT)
    out_ref[...] = value


def route_kernel(owner_col_ref, owner_row_ref, label_ref, place_ref):
    rows = owner_col_ref.shape[0]
    owner_row = owner_row_ref[...]
    earlier = lax.broadcasted_iota(jnp.int32, (rows, rows), 0) < lax.broadcasted_iota(jnp.int32, (rows, rows), 1)
    same = (owner_col_ref[...] == owner_row) & earlier
    rank = jnp.sum(same.astype(jnp.int32), axis=0, keepdims=True)
    target = owner_row * CAP + rank
    place_ref[...] = jnp.where(label_ref[...] == target, 1.0, 0.0).astype(BF)


def scatter_kernel(own_ref, got_ref, place_ref, out_ref):
    value = (own_ref[...] + got_ref[...].astype(F32)).astype(BF)
    out_ref[...] = dot(place_ref[...], value, NN).astype(BF)


def spread_order(count):
    groups = [int(g) for g in np.random.default_rng(1).permutation(count // 4)]
    return [4 * g + i for g in groups for i in range(4)]


def restore_kernel(from_ref, out_ref, *, home):
    rows = out_ref.shape[0] // len(home)
    for i, g in enumerate(home):
        out_ref[i * rows : (i + 1) * rows, :] = from_ref[g * rows : (g + 1) * rows, :]


def cost(flops, moved_bytes, exps=0):
    return pl.CostEstimate(flops=flops, bytes_accessed=moved_bytes, transcendentals=exps)


def on_device(query, key, value, out_grad, q_weight, k_weight, v_weight, adjacency, owner):
    rows, cols = query.shape
    half = cols // 2
    pair = 2 * HD
    sds = jax.ShapeDtypeStruct
    block = lax.axis_index("blk")
    ids = tuple(
        jnp.reshape(value, (1,)).astype(jnp.int32)
        for value in (block & 1, 1 - ((block >> 1) & 1), lax.axis_index("head"))
    )
    smem = pl.BlockSpec(memory_space=pltpu.SMEM)
    hbm = pl.BlockSpec(memory_space=pltpu.HBM)

    def call(kernel, outs, grid, in_specs, out_specs, scratch=(), placed=True, estimate=None, limit=16):
        return pl.pallas_call(
            functools.partial(with_place, kernel) if placed else kernel,
            out_shape=outs,
            grid_spec=pltpu.PrefetchScalarGridSpec(
                num_scalar_prefetch=3 if placed else 0, grid=grid, in_specs=in_specs, out_specs=out_specs,
                scratch_shapes=list(scratch),
            ),
            compiler_params=pltpu.CompilerParams(vmem_limit_bytes=limit << 20),
            cost_estimate=estimate,
        )

    def whole(*shape):
        return pl.BlockSpec(shape, lambda i, *p: (0,) * len(shape))

    packed = sds((rows + 16, 4 * half), BF)
    send, own = call(
        pack_kernel, (packed, packed), (1,), [hbm] * 5, (whole(rows + 16, 4 * half),) * 2,
        scratch=(pltpu.SMEM(adjacency.shape, jnp.int32), pltpu.SemaphoreType.DMA((9,))),
    )(*ids, *[pltpu.with_memory_space_constraint(x, pltpu.HBM) for x in (adjacency, key, value, query, out_grad)])
    got = core_swapped(send)
    kv_shape = sds((2, rows, half), BF)
    kv_whole = whole(2, rows, half)
    a, b, qg, bias = call(
        order_kernel,
        (kv_shape, kv_shape, sds((2, 2, rows, half), BF), sds((2, 16, rows), F32)),
        (1,),
        [whole(rows + 16, 4 * half)] * 2,
        (kv_whole, kv_whole, whole(2, 2, rows, half), whole(2, 16, rows)),
    )(*ids, own, got)
    ea = chip_swapped(a, 0)
    oa = chip_swapped(b, 1)
    eb = chip_swapped(b, 0)
    ob = chip_swapped(a, 1)
    ef = chip_swapped(oa, 0)
    of = chip_swapped(ea, 1)

    count = lax.axis_size("blk")
    slots = CAP * count
    order = spread_order(count)
    labels = jnp.asarray(np.array([[CAP * s + r] for s in order for r in range(CAP)], np.int32))
    place = call(
        route_kernel, sds((slots, rows), BF), (1,),
        [whole(rows, 1), whole(1, rows), whole(slots, 1)], whole(slots, rows), placed=False,
        estimate=cost(rows * rows * 8, 1 << 20),
    )(owner, owner.reshape(1, rows), labels)

    pairs = half // pair
    win = pl.BlockSpec((2, rows, pair), lambda i, *p: (0, 0, i))
    near = pl.BlockSpec((2, 2, rows, pair), lambda i, *p: (0, 0, 0, i))
    dq_spec = pl.BlockSpec((rows, pair), lambda i, *p: (0, i))
    stat_spec = pl.BlockSpec((2, 2, 8, rows), lambda i, *p: (0, i, 0, 0))
    bias_spec = whole(2, 16, rows)
    stat_shape = sds((2, 2 * pairs, 8, rows), F32)
    step = 2 * rows * rows * HD * 4
    part_shape = sds((pairs, 2, pair, rows), F32)
    part_spec = pl.BlockSpec((1, 2, pair, rows), lambda i, *p: (i, 0, 0, 0))

    def scratch(blocks):
        return (
            pltpu.VMEM((blocks * rows, 4 * rows), BF),
            pltpu.VMEM((blocks * rows, 4 * rows), BF),
            pltpu.VMEM((4 * rows, pair), BF),
            pltpu.VMEM((4 * rows, pair), BF),
            pltpu.VMEM((pair, blocks * rows), BF),
        )

    stats = call(
        first_stats_kernel, stat_shape, (pairs,), [win] * 4 + [near, bias_spec], stat_spec,
        estimate=cost(16 * step, 4 << 20),
    )(*ids, a, b, oa, ob, qg, bias)
    stats = call(
        second_stats_kernel, stat_shape, (pairs,), [win] * 2 + [near, bias_spec, stat_spec], stat_spec,
        estimate=cost(8 * step, 2 << 20),
    )(*ids, ea, eb, qg, bias, stats)
    stats, place = lax.optimization_barrier((stats, place))
    far_rows = pltpu.VMEM((2, 2 * rows, pair), BF)
    far_shape = sds((pairs, 2, rows, 2 * rows), BF)
    far_spec = pl.BlockSpec((1, 2, rows, 2 * rows), lambda i, *p: (i, 0, 0, 0))
    final, d_ef, d_of, ds_far = call(
        far_kernel, (stat_shape, kv_shape, kv_shape, far_shape), (pairs,),
        [win] * 2 + [near, bias_spec, stat_spec], (stat_spec, win, win, far_spec),
        scratch=(pltpu.VMEM((2, rows, 2 * rows), BF), far_rows, far_rows), estimate=cost(8 * step, 2 << 20),
    )(*ids, ef, of, qg, bias, stats)
    back_ef = chip_swapped(d_ef, 0)
    back_of = chip_swapped(d_of, 1)
    d_ea, d_oa, d_eb, d_ob, dq_near = call(
        near_kernel, (kv_shape,) * 4 + (part_shape,), (pairs,), [win] * 4 + [near, bias_spec, stat_spec],
        (win,) * 4 + (part_spec,), scratch=scratch(4), estimate=cost(32 * step, 4 << 20),
    )(*ids, ea, oa, eb, ob, qg, bias, final)
    back_eb = chip_swapped(d_eb, 0)
    back_ob = chip_swapped(d_ob, 1)
    back_ea = chip_swapped(joined(d_ea, back_of), 0)
    back_oa = chip_swapped(joined(d_oa, back_ef), 1)
    own_shape = sds((2, rows, half), F32)
    d_a, d_b, dq_own, dq_send = call(
        local_kernel, (own_shape, own_shape, sds((rows, half), BF), sds((rows, half), BF)), (pairs,),
        [win] * 4 + [near, bias_spec, stat_spec, part_spec, far_spec], (win, win, dq_spec, dq_spec),
        scratch=scratch(2), estimate=cost(16 * step, 4 << 20),
    )(*ids, a, b, ef, of, qg, bias, final, dq_near, ds_far)
    dq_got = core_swapped(dq_send)
    q_other, q_own = call(
        query_kernel, (sds((rows, cols), F32), sds((rows, cols), F32)), (1,),
        [whole(rows, half)] * 2 + [whole(2 * cols, cols)], (whole(rows, cols), whole(rows, cols)),
        estimate=cost(2 * rows * cols * 2 * cols, 3 << 20),
    )(*ids, dq_own, dq_got, q_weight)
    d_a, q_other, q_own = lax.optimization_barrier((d_a, q_other, q_own))
    keep, give = call(
        total_kernel, (kv_shape, kv_shape), (1,), [kv_whole] * 6, (kv_whole, kv_whole),
    )(*ids, d_a, d_b, back_ea, back_oa, back_eb, back_ob)
    gave = core_swapped(give)
    weight_keep = pl.BlockSpec((cols, half), lambda i, *p: (1 - p[2][0], p[0][0]))
    weight_gave = pl.BlockSpec((cols, half), lambda i, *p: (1 - p[2][0], 1 - p[0][0]))
    weight_own = pl.BlockSpec((cols, cols), lambda i, *p: (p[2][0], 0))
    add_cost = cost(2 * rows * cols * 2 * half, 2 << 20)
    partial_keep = call(
        add_kernel, sds((rows, cols), F32), (1,), [whole(rows, cols), kv_whole] + [weight_keep] * 2,
        whole(rows, cols), estimate=add_cost,
    )(*ids, q_other, keep, k_weight, v_weight)
    partial_other = call(
        add_kernel, sds((rows, cols), BF), (1,), [whole(rows, cols), kv_whole] + [weight_gave] * 2,
        whole(rows, cols), estimate=add_cost,
    )(*ids, partial_keep, gave, k_weight, v_weight)
    partial_got = lax.ppermute(partial_other, "head", [(0, 1), (1, 0)])
    partial_own = call(
        both_kernel, sds((rows, cols), F32), (1,),
        [whole(rows, cols)] + [kv_whole] * 2 + [weight_own] * 2, whole(rows, cols),
        estimate=cost(2 * rows * cols * 2 * cols, 2 << 20),
    )(*ids, q_own, keep, gave, k_weight, v_weight)
    outgoing = call(
        scatter_kernel, sds((slots, cols), BF), (1,),
        [whole(rows, cols), whole(rows, cols), whole(slots, rows)], whole(slots, cols), placed=False,
        estimate=cost(2 * slots * rows * cols, 2 << 20),
    )(partial_own, partial_got, place)
    arrived = lax.all_to_all(
        outgoing, "blk", split_axis=0, concat_axis=0, tiled=True, axis_index_groups=[order]
    )
    home = [int(g) for g in np.argsort(np.array(order[::4]) // 4)]
    return call(
        functools.partial(restore_kernel, home=home), sds((slots, cols), BF), (1,), [whole(slots, cols)],
        whole(slots, cols), placed=False,
    )(arrived)


def solution(mesh):
    return jax.shard_map(
        on_device,
        mesh=mesh,
        in_specs=(
            P("blk", "head"),
            P("blk", "head"),
            P("blk", "head"),
            P("blk", "head"),
            P(None, "head"),
            P(None, "head"),
            P(None, "head"),
            P("blk", None),
            P("blk", None),
        ),
        out_specs=P("blk", "head"),
        check_vma=False,
    )
```

```python
import functools
import math

import jax
import jax.numpy as jnp
import numpy as np
from jax import lax
from jax.experimental import pallas as pl
from jax.experimental.pallas import tpu as pltpu
from jax.sharding import PartitionSpec as P

HD = 64
BLOCK = 128
REACH = 3
SPAN = 2 * REACH + 1
LOG2E = math.log2(math.e)
MASKED = -1e30
FLOOR = -1e29
CAP = 4
BF = jnp.bfloat16
F32 = jnp.float32
NT = (((1,), (1,)), ((), ()))
NN = (((1,), (0,)), ((), ()))
TN = (((0,), (0,)), ((), ()))


def dot(a, b, dims):
    return lax.dot_general(a, b, dims, preferred_element_type=F32)


def core_swapped(value):
    count = lax.axis_size("blk")
    return lax.ppermute(value, "blk", [(s, s ^ 1) for s in range(count)])


def chip_swapped(value, odd):
    count = lax.axis_size("blk")
    ahead = [-2 if (s // 2) % 2 == odd else 2 for s in range(count)]
    return lax.ppermute(value, "blk", [(s, (s + ahead[s]) % count) for s in range(count)])


def bias_rows(adj_ref):
    shape = (16, 2 * BLOCK)
    row = lax.broadcasted_iota(jnp.int32, shape, 0)
    query_block = lax.broadcasted_iota(jnp.int32, shape, 1) // BLOCK
    allowed = row == 2 * REACH + query_block
    for c in range(2 * SPAN):
        for b in range(2):
            hit = (row == c) & (query_block == b) & (adj_ref[b, c] > 0)
            allowed = allowed | hit
    return jnp.where(allowed, 0.0, MASKED)


def with_place(kernel, core_ref, chip_ref, head_ref, *refs):
    kernel((core_ref[0], chip_ref[0], head_ref[0]), *refs)


def pack_kernel(ids, adj_in_ref, k_ref, v_ref, q_ref, g_ref, send_ref, own_ref, adj_ref, sems):
    rows, cols = k_ref.shape
    half = cols // 2
    copies = [pltpu.make_async_copy(adj_in_ref, adj_ref, sems.at[0])]
    for to_ref, which in ((send_ref, 1 - ids[0]), (own_ref, ids[0])):
        at = pl.ds(pl.multiple_of(which * half, half), half)
        for n, from_ref in enumerate((k_ref, v_ref, q_ref, g_ref)):
            copies.append(
                pltpu.make_async_copy(
                    from_ref.at[:, at], to_ref.at[0:rows, n * half : (n + 1) * half], sems.at[len(copies)]
                )
            )
    for copy in copies:
        copy.start()
    copies[0].wait()
    bias = bias_rows(adj_ref).astype(BF)
    for to_ref in (send_ref, own_ref):
        to_ref[rows : rows + 16, 0:half] = bias
        to_ref[rows : rows + 16, half:] = jnp.zeros((16, 3 * half), BF)
    for copy in copies[1:]:
        copy.wait()


def order_kernel(ids, own_ref, got_ref, a_ref, b_ref, qg_ref, bias_ref):
    rows = a_ref.shape[1]
    cols = a_ref.shape[2]
    par = ids[0]
    scale = 1.0 / math.sqrt(HD)
    for sector, from_ref in ((par, own_ref), (1 - par, got_ref)):
        qg_ref[0, sector] = from_ref[0:rows, 2 * cols : 3 * cols] * scale
        qg_ref[1, sector] = from_ref[0:rows, 3 * cols : 4 * cols]
        bias_ref[sector] = from_ref[rows : rows + 16, 0:cols].astype(F32)
    b_own = par == ids[1]
    for which in range(2):
        own = own_ref[0:rows, which * cols : (which + 1) * cols]
        got = got_ref[0:rows, which * cols : (which + 1) * cols]
        a_ref[which] = jnp.where(b_own, got, own)
        b_ref[which] = jnp.where(b_own, own, got)


def one_head(pair_ref, h):
    value = pair_ref[...]
    lane_head = lax.broadcasted_iota(jnp.int32, value.shape, 1) // HD
    return jnp.where(lane_head == h, value, 0.0).astype(BF)


def bias_pair_of(bias_ref, t, j):
    return [bias_ref[t, pl.ds(2 * j + b, 1), :] for b in range(2)]


def fold_stats(stats, key_value, query_head, grad_head, bias_pair):
    scores = dot(key_value[0], query_head, NT)
    grads = dot(key_value[1], grad_head, NT)
    top, total, delta = stats
    for b in range(2):
        at = slice(b * BLOCK, (b + 1) * BLOCK)
        new_top = jnp.maximum(top, jnp.max(scores[at], axis=0, keepdims=True) + bias_pair[b])
        weight = jnp.exp2(scores[at] * LOG2E + (bias_pair[b] - new_top) * LOG2E)
        shrink = jnp.exp2((top - new_top) * LOG2E)
        total = jnp.sum(weight, axis=0, keepdims=True) + total * shrink
        delta = jnp.sum(weight * grads[at], axis=0, keepdims=True) + delta * shrink
        top = new_top
    return (top, total, delta), scores, grads


def fold_windows(names, windows, qg_ref, bias_ref, before_ref, stats_ref):
    rows = qg_ref.shape[2]
    for t in range(2):
        for h in range(2):
            qh = one_head(qg_ref.at[0, t], h)
            gh = one_head(qg_ref.at[1, t], h)
            if before_ref is None:
                zero = jnp.zeros((1, rows), F32)
                stats = (zero + FLOOR, zero, zero)
            else:
                stats = tuple(before_ref[t, h, row : row + 1, :] for row in range(3))
            for w, window in zip(names, windows):
                stats, _, _ = fold_stats(stats, window, qh, gh, bias_pair_of(bias_ref, t, w - t))
            for row in range(3):
                stats_ref[t, h, row : row + 1, :] = stats[row]


def first_stats_kernel(ids, a_ref, b_ref, oa_ref, ob_ref, qg_ref, bias_ref, stats_ref):
    odd = ids[1]
    names = (4 - odd, 3 + odd, 2 + 3 * odd, 1 + 5 * odd)
    fold_windows(names, (a_ref, b_ref, oa_ref, ob_ref), qg_ref, bias_ref, None, stats_ref)


def second_stats_kernel(ids, ea_ref, eb_ref, qg_ref, bias_ref, before_ref, stats_ref):
    odd = ids[1]
    names = (5 - 3 * odd, 6 - 5 * odd)
    fold_windows(names, (ea_ref, eb_ref), qg_ref, bias_ref, before_ref, stats_ref)


def head_rows_of(first, second):
    row_head = lax.broadcasted_iota(jnp.int32, first.shape, 0) // HD
    return jnp.where(row_head == 0, first, second)


def query_grad(keys_t, grads, rows):
    both = dot(keys_t, grads, NN)
    return head_rows_of(both[:, 0:rows], both[:, rows:])


def flipped(value):
    return jnp.transpose(value.astype(F32)).astype(BF)


def far_kernel(
    ids, e_ref, o_ref, qg_ref, bias_ref, stats_ref, final_ref, de_ref, do_ref, ds_ref, ps_ref, qs_ref, gs_ref
):
    rows = qg_ref.shape[2]
    odd = ids[1]
    sides = ((1 - odd, e_ref, de_ref), (odd, o_ref, do_ref))
    halves = [slice(b * BLOCK, (b + 1) * BLOCK) for b in range(2)]
    pairs = qg_ref.shape[3] // (2 * HD)
    lanes = [slice(2 * HD * i, 2 * HD * (i + 1)) for i in range(pairs)]
    items = [(i, n, h) for i in range(pairs) for n in range(2) for h in range(2)]
    scores, grads, biases = [], [], []
    for i, n, h in items:
        t, window, _ = sides[n]
        cols = slice(h * rows, (h + 1) * rows)
        qh = one_head(qg_ref.at[0, t, :, lanes[i]], h)
        gh = one_head(qg_ref.at[1, t, :, lanes[i]], h)
        qs_ref[i, n, cols, :] = qh
        gs_ref[i, n, cols, :] = gh
        scores.append(dot(window[0, :, lanes[i]], qh, NT))
        grads.append(dot(window[1, :, lanes[i]], gh, NT))
        biases.append(bias_pair_of(bias_ref, t, (SPAN - 1) * t))
    before = [[stats_ref[sides[n][0], 2 * i + h, row : row + 1, :] for row in range(3)] for i, n, h in items]
    tops = []
    for value, bias, (top, _, _) in zip(scores, biases, before):
        for at, block_bias in zip(halves, bias):
            top = jnp.maximum(top, jnp.max(value[at], axis=0, keepdims=True) + block_bias)
        tops.append(top)
    weights, totals, deltas = [], [], []
    for value, grad, bias, top, (old, total, delta) in zip(scores, grads, biases, tops, before):
        shrink = jnp.exp2((old - top) * LOG2E)
        total = total * shrink
        delta = delta * shrink
        parts = []
        for at, block_bias in zip(halves, bias):
            weight = jnp.exp2(value[at] * LOG2E + (block_bias - top) * LOG2E)
            total = total + jnp.sum(weight, axis=0, keepdims=True)
            delta = delta + jnp.sum(weight * grad[at], axis=0, keepdims=True)
            parts.append(weight)
        weights.append(parts)
        totals.append(total)
        deltas.append(delta)
    for (i, n, h), parts, grad, top, total, delta in zip(items, weights, grads, tops, totals, deltas):
        cols = slice(h * rows, (h + 1) * rows)
        scale = 1.0 / total
        delta = delta * scale
        final_ref[sides[n][0], 2 * i + h, 0:1, :] = top * LOG2E + jnp.log2(total)
        final_ref[sides[n][0], 2 * i + h, 1:2, :] = delta
        for at, weight in zip(halves, parts):
            prob = weight * scale
            ps_ref[i, n, at, cols] = prob.astype(BF)
            ds_ref[i, n, at, cols] = (prob * (grad[at] - delta)).astype(BF)
    for i in range(pairs):
        for n in range(2):
            out_ref = sides[n][2]
            out_ref[0, :, lanes[i]] = dot(ds_ref[i, n], qs_ref[i, n], NN).astype(BF)
            out_ref[1, :, lanes[i]] = dot(ps_ref[i, n], gs_ref[i, n], NN).astype(BF)


def shared_kernel(names, qg_ref, bias_ref, final_ref, windows, outs, ps_ref, ds_ref, qs_ref, gs_ref, kt_ref):
    rows = qg_ref.shape[2]
    for t in range(2):
        for h in range(2):
            block = 2 * t + h
            cols = slice(block * rows, (block + 1) * rows)
            qs_ref[cols, :] = one_head(qg_ref.at[0, t], h)
            gs_ref[cols, :] = one_head(qg_ref.at[1, t], h)
    for n, (w, window) in enumerate(zip(names, windows)):
        keys = slice(n * rows, (n + 1) * rows)
        kt_ref[:, keys] = flipped(window[0])
        for t in range(2):
            for h in range(2):
                block = 2 * t + h
                cols = slice(block * rows, (block + 1) * rows)
                scores = dot(window[0], qs_ref[cols, :], NT)
                grads = dot(window[1], gs_ref[cols, :], NT)
                log_total = final_ref[t, h, 0:1, :]
                delta = final_ref[t, h, 1:2, :]
                bias_pair = bias_pair_of(bias_ref, t, w - t)
                for b in range(2):
                    at = slice(b * BLOCK, (b + 1) * BLOCK)
                    to = slice(n * rows + b * BLOCK, n * rows + (b + 1) * BLOCK)
                    prob = jnp.exp2(scores[at] * LOG2E + (bias_pair[b] * LOG2E - log_total))
                    ps_ref[to, cols] = prob.astype(BF)
                    ds_ref[to, cols] = (prob * (grads[at] - delta)).astype(BF)
        out_ref = outs[n]
        out_ref[0] = dot(ds_ref[keys, :], qs_ref[...], NN).astype(out_ref.dtype)
        out_ref[1] = dot(ps_ref[keys, :], gs_ref[...], NN).astype(out_ref.dtype)
    return [
        query_grad(kt_ref[...], ds_ref[:, 2 * t * rows : 2 * (t + 1) * rows], rows) for t in range(2)
    ]


def near_kernel(ids, ea_ref, oa_ref, eb_ref, ob_ref, qg_ref, bias_ref, final_ref, *refs):
    outs, dq_ref, scratch = refs[0:4], refs[4], refs[5:]
    odd = ids[1]
    names = (5 - 3 * odd, 2 + 3 * odd, 6 - 5 * odd, 1 + 5 * odd)
    grads = shared_kernel(names, qg_ref, bias_ref, final_ref, (ea_ref, oa_ref, eb_ref, ob_ref), outs, *scratch)
    for t in range(2):
        dq_ref[0, t] = grads[t]


def local_kernel(ids, a_ref, b_ref, ef_ref, of_ref, qg_ref, bias_ref, final_ref, part_ref, far_ref, *refs):
    outs, (dq_own_ref, dq_send_ref), scratch = refs[0:2], refs[2:4], refs[4:]
    rows = qg_ref.shape[2]
    odd = ids[1]
    grads = shared_kernel((4 - odd, 3 + odd), qg_ref, bias_ref, final_ref, (a_ref, b_ref), outs, *scratch)
    far_e = query_grad(flipped(ef_ref[0]), far_ref[0, 0], rows)
    far_o = query_grad(flipped(of_ref[0]), far_ref[0, 1], rows)
    even = odd == 0
    far = (jnp.where(even, far_o, far_e), jnp.where(even, far_e, far_o))
    total = [part_ref[0, t] + grads[t] + far[t] for t in range(2)]
    first = ids[0] == 0
    scale = 1.0 / math.sqrt(HD)
    dq_own_ref[...] = jnp.transpose(jnp.where(first, total[0], total[1]) * scale).astype(BF)
    dq_send_ref[...] = jnp.transpose(jnp.where(first, total[1], total[0]) * scale).astype(BF)


def joined(first, second):
    return (first.astype(F32) + second.astype(F32)).astype(BF)


def total_kernel(ids, a_ref, b_ref, ea_ref, oa_ref, eb_ref, ob_ref, keep_ref, send_ref):
    b_own = ids[0] == ids[1]
    for which in range(2):
        value_a = a_ref[which] + ob_ref[which].astype(F32) + ea_ref[which].astype(F32)
        value_b = b_ref[which] + eb_ref[which].astype(F32) + oa_ref[which].astype(F32)
        keep_ref[which] = jnp.where(b_own, value_b, value_a).astype(BF)
        send_ref[which] = jnp.where(b_own, value_a, value_b).astype(BF)


def query_kernel(ids, own_ref, got_ref, weight_ref, other_out_ref, own_out_ref):
    first = ids[0] == 0
    half = own_ref.shape[1]
    low = jnp.where(first, own_ref[...], got_ref[...])
    high = jnp.where(first, got_ref[...], own_ref[...])
    cols = own_out_ref.shape[1]
    here = ids[2]
    for out_ref, which in ((other_out_ref, 1 - here), (own_out_ref, here)):
        at = pl.ds(pl.multiple_of(which * cols, cols), cols)
        out_ref[...] = dot(low, weight_ref[at, 0:half], NT) + dot(high, weight_ref[at, half:], NT)


def add_kernel(ids, base_ref, grads_ref, wk_ref, wv_ref, out_ref):
    value = base_ref[...] + dot(grads_ref[0], wk_ref[...], NT) + dot(grads_ref[1], wv_ref[...], NT)
    out_ref[...] = value.astype(out_ref.dtype)


def both_kernel(ids, base_ref, keep_ref, gave_ref, wk_ref, wv_ref, out_ref):
    first = ids[0] == 0
    half = keep_ref.shape[2]
    value = base_ref[...]
    for which, weight in ((0, wk_ref), (1, wv_ref)):
        low = jnp.where(first, keep_ref[which], gave_ref[which])
        high = jnp.where(first, gave_ref[which], keep_ref[which])
        value = value + dot(low, weight[:, 0:half], NT) + dot(high, weight[:, half:], NT)
    out_ref[...] = value


def route_kernel(owner_col_ref, owner_row_ref, label_ref, place_ref):
    rows = owner_col_ref.shape[0]
    owner_row = owner_row_ref[...]
    earlier = lax.broadcasted_iota(jnp.int32, (rows, rows), 0) < lax.broadcasted_iota(jnp.int32, (rows, rows), 1)
    same = (owner_col_ref[...] == owner_row) & earlier
    rank = jnp.sum(same.astype(jnp.int32), axis=0, keepdims=True)
    target = owner_row * CAP + rank
    place_ref[...] = jnp.where(label_ref[...] == target, 1.0, 0.0).astype(BF)


def scatter_kernel(own_ref, got_ref, place_ref, out_ref):
    value = (own_ref[...] + got_ref[...].astype(F32)).astype(BF)
    out_ref[...] = dot(place_ref[...], value, NN).astype(BF)


def spread_order(count):
    groups = [int(g) for g in np.random.default_rng(1).permutation(count // 4)]
    return [4 * g + i for g in groups for i in range(4)]


def restore_kernel(from_ref, out_ref, *, home):
    rows = out_ref.shape[0] // len(home)
    for i, g in enumerate(home):
        out_ref[i * rows : (i + 1) * rows, :] = from_ref[g * rows : (g + 1) * rows, :]


def cost(flops, moved_bytes, exps=0):
    return pl.CostEstimate(flops=flops, bytes_accessed=moved_bytes, transcendentals=exps)


def on_device(query, key, value, out_grad, q_weight, k_weight, v_weight, adjacency, owner):
    rows, cols = query.shape
    half = cols // 2
    pair = 2 * HD
    sds = jax.ShapeDtypeStruct
    block = lax.axis_index("blk")
    ids = tuple(
        jnp.reshape(value, (1,)).astype(jnp.int32)
        for value in (block & 1, 1 - ((block >> 1) & 1), lax.axis_index("head"))
    )
    smem = pl.BlockSpec(memory_space=pltpu.SMEM)
    hbm = pl.BlockSpec(memory_space=pltpu.HBM)

    def call(kernel, outs, grid, in_specs, out_specs, scratch=(), placed=True, estimate=None, limit=16):
        return pl.pallas_call(
            functools.partial(with_place, kernel) if placed else kernel,
            out_shape=outs,
            grid_spec=pltpu.PrefetchScalarGridSpec(
                num_scalar_prefetch=3 if placed else 0, grid=grid, in_specs=in_specs, out_specs=out_specs,
                scratch_shapes=list(scratch),
            ),
            compiler_params=pltpu.CompilerParams(vmem_limit_bytes=limit << 20),
            cost_estimate=estimate,
        )

    def whole(*shape):
        return pl.BlockSpec(shape, lambda i, *p: (0,) * len(shape))

    packed = sds((rows + 16, 4 * half), BF)
    send, own = call(
        pack_kernel, (packed, packed), (1,), [hbm] * 5, (whole(rows + 16, 4 * half),) * 2,
        scratch=(pltpu.SMEM(adjacency.shape, jnp.int32), pltpu.SemaphoreType.DMA((9,))),
    )(*ids, *[pltpu.with_memory_space_constraint(x, pltpu.HBM) for x in (adjacency, key, value, query, out_grad)])
    got = core_swapped(send)
    kv_shape = sds((2, rows, half), BF)
    kv_whole = whole(2, rows, half)
    a, b, qg, bias = call(
        order_kernel,
        (kv_shape, kv_shape, sds((2, 2, rows, half), BF), sds((2, 16, rows), F32)),
        (1,),
        [whole(rows + 16, 4 * half)] * 2,
        (kv_whole, kv_whole, whole(2, 2, rows, half), whole(2, 16, rows)),
    )(*ids, own, got)
    ea = chip_swapped(a, 0)
    oa = chip_swapped(b, 1)
    eb = chip_swapped(b, 0)
    ob = chip_swapped(a, 1)
    ef = chip_swapped(oa, 0)
    of = chip_swapped(ea, 1)

    count = lax.axis_size("blk")
    slots = CAP * count
    order = spread_order(count)
    labels = jnp.asarray(np.array([[CAP * s + r] for s in order for r in range(CAP)], np.int32))
    place = call(
        route_kernel, sds((slots, rows), BF), (1,),
        [whole(rows, 1), whole(1, rows), whole(slots, 1)], whole(slots, rows), placed=False,
        estimate=cost(rows * rows * 8, 1 << 20),
    )(owner, owner.reshape(1, rows), labels)

    pairs = half // pair
    win = pl.BlockSpec((2, rows, pair), lambda i, *p: (0, 0, i))
    near = pl.BlockSpec((2, 2, rows, pair), lambda i, *p: (0, 0, 0, i))
    dq_spec = pl.BlockSpec((rows, pair), lambda i, *p: (0, i))
    stat_spec = pl.BlockSpec((2, 2, 8, rows), lambda i, *p: (0, i, 0, 0))
    bias_spec = whole(2, 16, rows)
    stat_shape = sds((2, 2 * pairs, 8, rows), F32)
    step = 2 * rows * rows * HD * 4
    part_shape = sds((pairs, 2, pair, rows), F32)
    part_spec = pl.BlockSpec((1, 2, pair, rows), lambda i, *p: (i, 0, 0, 0))

    def scratch(blocks):
        return (
            pltpu.VMEM((blocks * rows, 4 * rows), BF),
            pltpu.VMEM((blocks * rows, 4 * rows), BF),
            pltpu.VMEM((4 * rows, pair), BF),
            pltpu.VMEM((4 * rows, pair), BF),
            pltpu.VMEM((pair, blocks * rows), BF),
        )

    stats = call(
        first_stats_kernel, stat_shape, (pairs,), [win] * 4 + [near, bias_spec], stat_spec,
        estimate=cost(16 * step, 4 << 20),
    )(*ids, a, b, oa, ob, qg, bias)
    stats = call(
        second_stats_kernel, stat_shape, (pairs,), [win] * 2 + [near, bias_spec, stat_spec], stat_spec,
        estimate=cost(8 * step, 2 << 20),
    )(*ids, ea, eb, qg, bias, stats)
    stats, place = lax.optimization_barrier((stats, place))
    far_rows = pltpu.VMEM((pairs, 2, 2 * rows, pair), BF)
    far_shape = sds((pairs, 2, rows, 2 * rows), BF)
    far_spec = pl.BlockSpec((1, 2, rows, 2 * rows), lambda i, *p: (i, 0, 0, 0))
    stat_whole = whole(2, 2 * pairs, 8, rows)
    final, d_ef, d_of, ds_far = call(
        far_kernel, (stat_shape, kv_shape, kv_shape, far_shape), (1,),
        [kv_whole] * 2 + [whole(2, 2, rows, half), bias_spec, stat_whole],
        (stat_whole, kv_whole, kv_whole, whole(pairs, 2, rows, 2 * rows)),
        scratch=(pltpu.VMEM((pairs, 2, rows, 2 * rows), BF), far_rows, far_rows), estimate=cost(8 * step, 2 << 20),
    )(*ids, ef, of, qg, bias, stats)
    back_ef = chip_swapped(d_ef, 0)
    back_of = chip_swapped(d_of, 1)
    d_ea, d_oa, d_eb, d_ob, dq_near = call(
        near_kernel, (kv_shape,) * 4 + (part_shape,), (pairs,), [win] * 4 + [near, bias_spec, stat_spec],
        (win,) * 4 + (part_spec,), scratch=scratch(4), estimate=cost(32 * step, 4 << 20),
    )(*ids, ea, oa, eb, ob, qg, bias, final)
    back_eb = chip_swapped(d_eb, 0)
    back_ob = chip_swapped(d_ob, 1)
    back_ea = chip_swapped(joined(d_ea, back_of), 0)
    back_oa = chip_swapped(joined(d_oa, back_ef), 1)
    own_shape = sds((2, rows, half), F32)
    d_a, d_b, dq_own, dq_send = call(
        local_kernel, (own_shape, own_shape, sds((rows, half), BF), sds((rows, half), BF)), (pairs,),
        [win] * 4 + [near, bias_spec, stat_spec, part_spec, far_spec], (win, win, dq_spec, dq_spec),
        scratch=scratch(2), estimate=cost(16 * step, 4 << 20),
    )(*ids, a, b, ef, of, qg, bias, final, dq_near, ds_far)
    dq_got = core_swapped(dq_send)
    q_other, q_own = call(
        query_kernel, (sds((rows, cols), F32), sds((rows, cols), F32)), (1,),
        [whole(rows, half)] * 2 + [whole(2 * cols, cols)], (whole(rows, cols), whole(rows, cols)),
        estimate=cost(2 * rows * cols * 2 * cols, 3 << 20),
    )(*ids, dq_own, dq_got, q_weight)
    d_a, q_other, q_own = lax.optimization_barrier((d_a, q_other, q_own))
    keep, give = call(
        total_kernel, (kv_shape, kv_shape), (1,), [kv_whole] * 6, (kv_whole, kv_whole),
    )(*ids, d_a, d_b, back_ea, back_oa, back_eb, back_ob)
    gave = core_swapped(give)
    weight_keep = pl.BlockSpec((cols, half), lambda i, *p: (1 - p[2][0], p[0][0]))
    weight_gave = pl.BlockSpec((cols, half), lambda i, *p: (1 - p[2][0], 1 - p[0][0]))
    weight_own = pl.BlockSpec((cols, cols), lambda i, *p: (p[2][0], 0))
    add_cost = cost(2 * rows * cols * 2 * half, 2 << 20)
    partial_keep = call(
        add_kernel, sds((rows, cols), F32), (1,), [whole(rows, cols), kv_whole] + [weight_keep] * 2,
        whole(rows, cols), estimate=add_cost,
    )(*ids, q_other, keep, k_weight, v_weight)
    partial_other = call(
        add_kernel, sds((rows, cols), BF), (1,), [whole(rows, cols), kv_whole] + [weight_gave] * 2,
        whole(rows, cols), estimate=add_cost,
    )(*ids, partial_keep, gave, k_weight, v_weight)
    partial_got = lax.ppermute(partial_other, "head", [(0, 1), (1, 0)])
    partial_own = call(
        both_kernel, sds((rows, cols), F32), (1,),
        [whole(rows, cols)] + [kv_whole] * 2 + [weight_own] * 2, whole(rows, cols),
        estimate=cost(2 * rows * cols * 2 * cols, 2 << 20),
    )(*ids, q_own, keep, gave, k_weight, v_weight)
    outgoing = call(
        scatter_kernel, sds((slots, cols), BF), (1,),
        [whole(rows, cols), whole(rows, cols), whole(slots, rows)], whole(slots, cols), placed=False,
        estimate=cost(2 * slots * rows * cols, 2 << 20),
    )(partial_own, partial_got, place)
    arrived = lax.all_to_all(
        outgoing, "blk", split_axis=0, concat_axis=0, tiled=True, axis_index_groups=[order]
    )
    home = [int(g) for g in np.argsort(np.array(order[::4]) // 4)]
    return call(
        functools.partial(restore_kernel, home=home), sds((slots, cols), BF), (1,), [whole(slots, cols)],
        whole(slots, cols), placed=False,
    )(arrived)


def solution(mesh):
    return jax.shard_map(
        on_device,
        mesh=mesh,
        in_specs=(
            P("blk", "head"),
            P("blk", "head"),
            P("blk", "head"),
            P("blk", "head"),
            P(None, "head"),
            P(None, "head"),
            P(None, "head"),
            P("blk", None),
            P("blk", None),
        ),
        out_specs=P("blk", "head"),
        check_vma=False,
    )
```

```python
import functools
import math

import jax
import jax.numpy as jnp
import numpy as np
from jax import lax
from jax.experimental import pallas as pl
from jax.experimental.pallas import tpu as pltpu
from jax.sharding import PartitionSpec as P

HD = 64
BLOCK = 128
REACH = 3
SPAN = 2 * REACH + 1
LOG2E = math.log2(math.e)
MASKED = -1e30
FLOOR = -1e29
CAP = 4
BF = jnp.bfloat16
F32 = jnp.float32
NT = (((1,), (1,)), ((), ()))
NN = (((1,), (0,)), ((), ()))
TN = (((0,), (0,)), ((), ()))


def dot(a, b, dims):
    return lax.dot_general(a, b, dims, preferred_element_type=F32)


def core_swapped(value):
    count = lax.axis_size("blk")
    return lax.ppermute(value, "blk", [(s, s ^ 1) for s in range(count)])


def chip_swapped(value, odd):
    count = lax.axis_size("blk")
    ahead = [-2 if (s // 2) % 2 == odd else 2 for s in range(count)]
    return lax.ppermute(value, "blk", [(s, (s + ahead[s]) % count) for s in range(count)])


def bias_rows(adj_ref):
    shape = (16, 2 * BLOCK)
    row = lax.broadcasted_iota(jnp.int32, shape, 0)
    query_block = lax.broadcasted_iota(jnp.int32, shape, 1) // BLOCK
    allowed = row == 2 * REACH + query_block
    for c in range(2 * SPAN):
        for b in range(2):
            hit = (row == c) & (query_block == b) & (adj_ref[b, c] > 0)
            allowed = allowed | hit
    return jnp.where(allowed, 0.0, MASKED)


def with_place(kernel, core_ref, chip_ref, head_ref, *refs):
    kernel((core_ref[0], chip_ref[0], head_ref[0]), *refs)


def pack_kernel(ids, adj_in_ref, k_ref, v_ref, q_ref, g_ref, send_kv_ref, own_kv_ref, send_qg_ref, own_qg_ref, adj_ref, sems):
    rows, cols = k_ref.shape
    half = cols // 2
    copies = []
    for kv_ref, qg_ref, which in ((send_kv_ref, send_qg_ref, 1 - ids[0]), (own_kv_ref, own_qg_ref, ids[0])):
        at = pl.ds(pl.multiple_of(which * half, half), half)
        for n, from_ref in enumerate((k_ref, v_ref)):
            copies.append(pltpu.make_async_copy(from_ref.at[:, at], kv_ref.at[n], sems.at[len(copies)]))
        for n, from_ref in enumerate((q_ref, g_ref)):
            to = qg_ref.at[0:rows, n * half : (n + 1) * half]
            copies.append(pltpu.make_async_copy(from_ref.at[:, at], to, sems.at[len(copies)]))
    adjacency = pltpu.make_async_copy(adj_in_ref, adj_ref, sems.at[len(copies)])
    adjacency.start()
    for copy in copies:
        copy.start()
    adjacency.wait()
    bias = bias_rows(adj_ref).astype(BF)
    for to_ref in (send_qg_ref, own_qg_ref):
        to_ref[rows : rows + 16, 0:half] = bias
        to_ref[rows : rows + 16, half:] = jnp.zeros((16, half), BF)
    for copy in copies:
        copy.wait()


def order_keys_kernel(ids, own_ref, got_ref, a_ref, b_ref):
    b_own = ids[0] == ids[1]
    own = own_ref[...]
    got = got_ref[...]
    a_ref[...] = jnp.where(b_own, got, own)
    b_ref[...] = jnp.where(b_own, own, got)


def order_queries_kernel(ids, own_ref, got_ref, qg_ref, bias_ref):
    rows, cols = qg_ref.shape[2:]
    scale = 1.0 / math.sqrt(HD)
    for sector, from_ref in ((ids[0], own_ref), (1 - ids[0], got_ref)):
        qg_ref[0, sector] = from_ref[0:rows, 0:cols] * scale
        qg_ref[1, sector] = from_ref[0:rows, cols : 2 * cols]
        bias_ref[sector] = from_ref[rows : rows + 16, 0:cols].astype(F32)


def one_head(pair_ref, h):
    value = pair_ref[...]
    lane_head = lax.broadcasted_iota(jnp.int32, value.shape, 1) // HD
    return jnp.where(lane_head == h, value, 0.0).astype(BF)


def bias_pair_of(bias_ref, t, j):
    return [bias_ref[t, pl.ds(2 * j + b, 1), :] for b in range(2)]


def fold_stats(stats, key_value, query_head, grad_head, bias_pair):
    scores = dot(key_value[0], query_head, NT)
    grads = dot(key_value[1], grad_head, NT)
    top, total, delta = stats
    for b in range(2):
        at = slice(b * BLOCK, (b + 1) * BLOCK)
        new_top = jnp.maximum(top, jnp.max(scores[at], axis=0, keepdims=True) + bias_pair[b])
        weight = jnp.exp2(scores[at] * LOG2E + (bias_pair[b] - new_top) * LOG2E)
        shrink = jnp.exp2((top - new_top) * LOG2E)
        total = jnp.sum(weight, axis=0, keepdims=True) + total * shrink
        delta = jnp.sum(weight * grads[at], axis=0, keepdims=True) + delta * shrink
        top = new_top
    return (top, total, delta), scores, grads


def fold_windows(names, windows, qg_ref, bias_ref, before_ref, stats_ref):
    rows = qg_ref.shape[2]
    for t in range(2):
        for h in range(2):
            qh = one_head(qg_ref.at[0, t], h)
            gh = one_head(qg_ref.at[1, t], h)
            if before_ref is None:
                zero = jnp.zeros((1, rows), F32)
                stats = (zero + FLOOR, zero, zero)
            else:
                stats = tuple(before_ref[t, h, row : row + 1, :] for row in range(3))
            for w, window in zip(names, windows):
                stats, _, _ = fold_stats(stats, window, qh, gh, bias_pair_of(bias_ref, t, w - t))
            for row in range(3):
                stats_ref[t, h, row : row + 1, :] = stats[row]


def first_stats_kernel(ids, a_ref, b_ref, oa_ref, ob_ref, qg_ref, bias_ref, stats_ref):
    odd = ids[1]
    names = (4 - odd, 3 + odd, 2 + 3 * odd, 1 + 5 * odd)
    fold_windows(names, (a_ref, b_ref, oa_ref, ob_ref), qg_ref, bias_ref, None, stats_ref)


def second_stats_kernel(ids, ea_ref, eb_ref, qg_ref, bias_ref, before_ref, stats_ref):
    odd = ids[1]
    names = (5 - 3 * odd, 6 - 5 * odd)
    fold_windows(names, (ea_ref, eb_ref), qg_ref, bias_ref, before_ref, stats_ref)


def head_rows_of(first, second):
    row_head = lax.broadcasted_iota(jnp.int32, first.shape, 0) // HD
    return jnp.where(row_head == 0, first, second)


def query_grad(keys_t, grads, rows):
    both = dot(keys_t, grads, NN)
    return head_rows_of(both[:, 0:rows], both[:, rows:])


def flipped(value):
    return jnp.transpose(value.astype(F32)).astype(BF)


def far_kernel(
    ids, e_ref, o_ref, qg_ref, bias_ref, stats_ref, final_ref, de_ref, do_ref, ds_ref, ps_ref, qs_ref, gs_ref
):
    rows = qg_ref.shape[2]
    odd = ids[1]
    sides = ((1 - odd, e_ref, de_ref), (odd, o_ref, do_ref))
    halves = [slice(b * BLOCK, (b + 1) * BLOCK) for b in range(2)]
    pairs = qg_ref.shape[3] // (2 * HD)
    lanes = [slice(2 * HD * i, 2 * HD * (i + 1)) for i in range(pairs)]
    items = [(i, n, h) for i in range(pairs) for n in range(2) for h in range(2)]
    scores, grads, biases = [], [], []
    for i, n, h in items:
        t, window, _ = sides[n]
        cols = slice(h * rows, (h + 1) * rows)
        qh = one_head(qg_ref.at[0, t, :, lanes[i]], h)
        gh = one_head(qg_ref.at[1, t, :, lanes[i]], h)
        qs_ref[i, n, cols, :] = qh
        gs_ref[i, n, cols, :] = gh
        scores.append(dot(window[0, :, lanes[i]], qh, NT))
        grads.append(dot(window[1, :, lanes[i]], gh, NT))
        biases.append(bias_pair_of(bias_ref, t, (SPAN - 1) * t))
    before = [[stats_ref[sides[n][0], 2 * i + h, row : row + 1, :] for row in range(3)] for i, n, h in items]
    tops = []
    for value, bias, (top, _, _) in zip(scores, biases, before):
        for at, block_bias in zip(halves, bias):
            top = jnp.maximum(top, jnp.max(value[at], axis=0, keepdims=True) + block_bias)
        tops.append(top)
    weights, totals, deltas = [], [], []
    for value, grad, bias, top, (old, total, delta) in zip(scores, grads, biases, tops, before):
        shrink = jnp.exp2((old - top) * LOG2E)
        total = total * shrink
        delta = delta * shrink
        parts = []
        for at, block_bias in zip(halves, bias):
            weight = jnp.exp2(value[at] * LOG2E + (block_bias - top) * LOG2E)
            total = total + jnp.sum(weight, axis=0, keepdims=True)
            delta = delta + jnp.sum(weight * grad[at], axis=0, keepdims=True)
            parts.append(weight)
        weights.append(parts)
        totals.append(total)
        deltas.append(delta)
    for (i, n, h), parts, grad, top, total, delta in zip(items, weights, grads, tops, totals, deltas):
        cols = slice(h * rows, (h + 1) * rows)
        scale = 1.0 / total
        delta = delta * scale
        final_ref[sides[n][0], 2 * i + h, 0:1, :] = top * LOG2E + jnp.log2(total)
        final_ref[sides[n][0], 2 * i + h, 1:2, :] = delta
        for at, weight in zip(halves, parts):
            prob = weight * scale
            ps_ref[i, n, at, cols] = prob.astype(BF)
            ds_ref[i, n, at, cols] = (prob * (grad[at] - delta)).astype(BF)
    for i in range(pairs):
        for n in range(2):
            out_ref = sides[n][2]
            out_ref[0, :, lanes[i]] = dot(ds_ref[i, n], qs_ref[i, n], NN).astype(BF)
            out_ref[1, :, lanes[i]] = dot(ps_ref[i, n], gs_ref[i, n], NN).astype(BF)


def shared_kernel(names, qg_ref, bias_ref, final_ref, windows, outs, ps_ref, ds_ref, qs_ref, gs_ref, kt_ref):
    rows = qg_ref.shape[2]
    for t in range(2):
        for h in range(2):
            block = 2 * t + h
            cols = slice(block * rows, (block + 1) * rows)
            qs_ref[cols, :] = one_head(qg_ref.at[0, t], h)
            gs_ref[cols, :] = one_head(qg_ref.at[1, t], h)
    for n, (w, window) in enumerate(zip(names, windows)):
        keys = slice(n * rows, (n + 1) * rows)
        kt_ref[:, keys] = flipped(window[0])
        for t in range(2):
            for h in range(2):
                block = 2 * t + h
                cols = slice(block * rows, (block + 1) * rows)
                scores = dot(window[0], qs_ref[cols, :], NT)
                grads = dot(window[1], gs_ref[cols, :], NT)
                log_total = final_ref[t, h, 0:1, :]
                delta = final_ref[t, h, 1:2, :]
                bias_pair = bias_pair_of(bias_ref, t, w - t)
                for b in range(2):
                    at = slice(b * BLOCK, (b + 1) * BLOCK)
                    to = slice(n * rows + b * BLOCK, n * rows + (b + 1) * BLOCK)
                    prob = jnp.exp2(scores[at] * LOG2E + (bias_pair[b] * LOG2E - log_total))
                    ps_ref[to, cols] = prob.astype(BF)
                    ds_ref[to, cols] = (prob * (grads[at] - delta)).astype(BF)
        out_ref = outs[n]
        out_ref[0] = dot(ds_ref[keys, :], qs_ref[...], NN).astype(out_ref.dtype)
        out_ref[1] = dot(ps_ref[keys, :], gs_ref[...], NN).astype(out_ref.dtype)
    return [
        query_grad(kt_ref[...], ds_ref[:, 2 * t * rows : 2 * (t + 1) * rows], rows) for t in range(2)
    ]


def near_kernel(ids, ea_ref, oa_ref, eb_ref, ob_ref, qg_ref, bias_ref, final_ref, *refs):
    outs, dq_ref, scratch = refs[0:4], refs[4], refs[5:]
    odd = ids[1]
    names = (5 - 3 * odd, 2 + 3 * odd, 6 - 5 * odd, 1 + 5 * odd)
    grads = shared_kernel(names, qg_ref, bias_ref, final_ref, (ea_ref, oa_ref, eb_ref, ob_ref), outs, *scratch)
    for t in range(2):
        dq_ref[0, t] = grads[t]


def local_kernel(ids, a_ref, b_ref, ef_ref, of_ref, qg_ref, bias_ref, final_ref, part_ref, far_ref, *refs):
    outs, (dq_own_ref, dq_send_ref), scratch = refs[0:2], refs[2:4], refs[4:]
    rows = qg_ref.shape[2]
    odd = ids[1]
    grads = shared_kernel((4 - odd, 3 + odd), qg_ref, bias_ref, final_ref, (a_ref, b_ref), outs, *scratch)
    far_e = query_grad(flipped(ef_ref[0]), far_ref[0, 0], rows)
    far_o = query_grad(flipped(of_ref[0]), far_ref[0, 1], rows)
    even = odd == 0
    far = (jnp.where(even, far_o, far_e), jnp.where(even, far_e, far_o))
    total = [part_ref[0, t] + grads[t] + far[t] for t in range(2)]
    first = ids[0] == 0
    scale = 1.0 / math.sqrt(HD)
    dq_own_ref[...] = jnp.transpose(jnp.where(first, total[0], total[1]) * scale).astype(BF)
    dq_send_ref[...] = jnp.transpose(jnp.where(first, total[1], total[0]) * scale).astype(BF)


def joined(first, second):
    return (first.astype(F32) + second.astype(F32)).astype(BF)


def total_kernel(ids, a_ref, b_ref, ea_ref, oa_ref, eb_ref, ob_ref, keep_ref, send_ref):
    b_own = ids[0] == ids[1]
    for which in range(2):
        value_a = a_ref[which] + ob_ref[which].astype(F32) + ea_ref[which].astype(F32)
        value_b = b_ref[which] + eb_ref[which].astype(F32) + oa_ref[which].astype(F32)
        keep_ref[which] = jnp.where(b_own, value_b, value_a).astype(BF)
        send_ref[which] = jnp.where(b_own, value_a, value_b).astype(BF)


def query_kernel(ids, own_ref, got_ref, weight_ref, other_out_ref, own_out_ref):
    first = ids[0] == 0
    half = own_ref.shape[1]
    low = jnp.where(first, own_ref[...], got_ref[...])
    high = jnp.where(first, got_ref[...], own_ref[...])
    cols = own_out_ref.shape[1]
    here = ids[2]
    for out_ref, which in ((other_out_ref, 1 - here), (own_out_ref, here)):
        at = pl.ds(pl.multiple_of(which * cols, cols), cols)
        out_ref[...] = dot(low, weight_ref[at, 0:half], NT) + dot(high, weight_ref[at, half:], NT)


def add_kernel(ids, base_ref, grads_ref, wk_ref, wv_ref, out_ref):
    value = base_ref[...] + dot(grads_ref[0], wk_ref[...], NT) + dot(grads_ref[1], wv_ref[...], NT)
    out_ref[...] = value.astype(out_ref.dtype)


def both_kernel(ids, base_ref, keep_ref, gave_ref, wk_ref, wv_ref, out_ref):
    first = ids[0] == 0
    half = keep_ref.shape[2]
    value = base_ref[...]
    for which, weight in ((0, wk_ref), (1, wv_ref)):
        low = jnp.where(first, keep_ref[which], gave_ref[which])
        high = jnp.where(first, gave_ref[which], keep_ref[which])
        value = value + dot(low, weight[:, 0:half], NT) + dot(high, weight[:, half:], NT)
    out_ref[...] = value


def route_kernel(owner_col_ref, owner_row_ref, label_ref, place_ref):
    rows = owner_col_ref.shape[0]
    owner_row = owner_row_ref[...]
    earlier = lax.broadcasted_iota(jnp.int32, (rows, rows), 0) < lax.broadcasted_iota(jnp.int32, (rows, rows), 1)
    same = (owner_col_ref[...] == owner_row) & earlier
    rank = jnp.sum(same.astype(jnp.int32), axis=0, keepdims=True)
    target = owner_row * CAP + rank
    place_ref[...] = jnp.where(label_ref[...] == target, 1.0, 0.0).astype(BF)


def scatter_kernel(own_ref, got_ref, place_ref, out_ref):
    value = (own_ref[...] + got_ref[...].astype(F32)).astype(BF)
    out_ref[...] = dot(place_ref[...], value, NN).astype(BF)


def spread_order(count):
    groups = [int(g) for g in np.random.default_rng(1).permutation(count // 4)]
    return [4 * g + i for g in groups for i in range(4)]


def restore_kernel(from_ref, out_ref, *, home):
    rows = out_ref.shape[0] // len(home)
    for i, g in enumerate(home):
        out_ref[i * rows : (i + 1) * rows, :] = from_ref[g * rows : (g + 1) * rows, :]


def cost(flops, moved_bytes, exps=0):
    return pl.CostEstimate(flops=flops, bytes_accessed=moved_bytes, transcendentals=exps)


def on_device(query, key, value, out_grad, q_weight, k_weight, v_weight, adjacency, owner):
    rows, cols = query.shape
    half = cols // 2
    pair = 2 * HD
    sds = jax.ShapeDtypeStruct
    block = lax.axis_index("blk")
    ids = tuple(
        jnp.reshape(value, (1,)).astype(jnp.int32)
        for value in (block & 1, 1 - ((block >> 1) & 1), lax.axis_index("head"))
    )
    smem = pl.BlockSpec(memory_space=pltpu.SMEM)
    hbm = pl.BlockSpec(memory_space=pltpu.HBM)

    def call(kernel, outs, grid, in_specs, out_specs, scratch=(), placed=True, estimate=None, limit=16):
        return pl.pallas_call(
            functools.partial(with_place, kernel) if placed else kernel,
            out_shape=outs,
            grid_spec=pltpu.PrefetchScalarGridSpec(
                num_scalar_prefetch=3 if placed else 0, grid=grid, in_specs=in_specs, out_specs=out_specs,
                scratch_shapes=list(scratch),
            ),
            compiler_params=pltpu.CompilerParams(vmem_limit_bytes=limit << 20),
            cost_estimate=estimate,
        )

    def whole(*shape):
        return pl.BlockSpec(shape, lambda i, *p: (0,) * len(shape))

    kv_shape = sds((2, rows, half), BF)
    kv_whole = whole(2, rows, half)
    qg_packed = sds((rows + 16, 2 * half), BF)
    packed_whole = whole(rows + 16, 2 * half)
    send_kv, own_kv, send_qg, own_qg = call(
        pack_kernel, (kv_shape, kv_shape, qg_packed, qg_packed), (1,), [hbm] * 5,
        (kv_whole, kv_whole, packed_whole, packed_whole),
        scratch=(pltpu.SMEM(adjacency.shape, jnp.int32), pltpu.SemaphoreType.DMA((9,))),
    )(*ids, *[pltpu.with_memory_space_constraint(x, pltpu.HBM) for x in (adjacency, key, value, query, out_grad)])
    got_kv = core_swapped(send_kv)
    a, b = call(order_keys_kernel, (kv_shape, kv_shape), (1,), [kv_whole] * 2, (kv_whole, kv_whole))(
        *ids, own_kv, got_kv
    )
    send_qg, a, b = lax.optimization_barrier((send_qg, a, b))
    got_qg = core_swapped(send_qg)
    qg, bias = call(
        order_queries_kernel, (sds((2, 2, rows, half), BF), sds((2, 16, rows), F32)), (1,),
        [packed_whole] * 2, (whole(2, 2, rows, half), whole(2, 16, rows)),
    )(*ids, own_qg, got_qg)
    ea = chip_swapped(a, 0)
    oa = chip_swapped(b, 1)
    eb = chip_swapped(b, 0)
    ob = chip_swapped(a, 1)
    ef = chip_swapped(oa, 0)
    of = chip_swapped(ea, 1)

    count = lax.axis_size("blk")
    slots = CAP * count
    order = spread_order(count)
    labels = jnp.asarray(np.array([[CAP * s + r] for s in order for r in range(CAP)], np.int32))
    place = call(
        route_kernel, sds((slots, rows), BF), (1,),
        [whole(rows, 1), whole(1, rows), whole(slots, 1)], whole(slots, rows), placed=False,
        estimate=cost(rows * rows * 8, 1 << 20),
    )(owner, owner.reshape(1, rows), labels)

    pairs = half // pair
    win = pl.BlockSpec((2, rows, pair), lambda i, *p: (0, 0, i))
    near = pl.BlockSpec((2, 2, rows, pair), lambda i, *p: (0, 0, 0, i))
    dq_spec = pl.BlockSpec((rows, pair), lambda i, *p: (0, i))
    stat_spec = pl.BlockSpec((2, 2, 8, rows), lambda i, *p: (0, i, 0, 0))
    bias_spec = whole(2, 16, rows)
    stat_shape = sds((2, 2 * pairs, 8, rows), F32)
    step = 2 * rows * rows * HD * 4
    part_shape = sds((pairs, 2, pair, rows), F32)
    part_spec = pl.BlockSpec((1, 2, pair, rows), lambda i, *p: (i, 0, 0, 0))

    def scratch(blocks):
        return (
            pltpu.VMEM((blocks * rows, 4 * rows), BF),
            pltpu.VMEM((blocks * rows, 4 * rows), BF),
            pltpu.VMEM((4 * rows, pair), BF),
            pltpu.VMEM((4 * rows, pair), BF),
            pltpu.VMEM((pair, blocks * rows), BF),
        )

    stats = call(
        first_stats_kernel, stat_shape, (pairs,), [win] * 4 + [near, bias_spec], stat_spec,
        estimate=cost(16 * step, 4 << 20),
    )(*ids, a, b, oa, ob, qg, bias)
    stats = call(
        second_stats_kernel, stat_shape, (pairs,), [win] * 2 + [near, bias_spec, stat_spec], stat_spec,
        estimate=cost(8 * step, 2 << 20),
    )(*ids, ea, eb, qg, bias, stats)
    stats, place = lax.optimization_barrier((stats, place))
    far_rows = pltpu.VMEM((pairs, 2, 2 * rows, pair), BF)
    far_shape = sds((pairs, 2, rows, 2 * rows), BF)
    far_spec = pl.BlockSpec((1, 2, rows, 2 * rows), lambda i, *p: (i, 0, 0, 0))
    stat_whole = whole(2, 2 * pairs, 8, rows)
    final, d_ef, d_of, ds_far = call(
        far_kernel, (stat_shape, kv_shape, kv_shape, far_shape), (1,),
        [kv_whole] * 2 + [whole(2, 2, rows, half), bias_spec, stat_whole],
        (stat_whole, kv_whole, kv_whole, whole(pairs, 2, rows, 2 * rows)),
        scratch=(pltpu.VMEM((pairs, 2, rows, 2 * rows), BF), far_rows, far_rows), estimate=cost(8 * step, 2 << 20),
    )(*ids, ef, of, qg, bias, stats)
    back_ef = chip_swapped(d_ef, 0)
    back_of = chip_swapped(d_of, 1)
    d_ea, d_oa, d_eb, d_ob, dq_near = call(
        near_kernel, (kv_shape,) * 4 + (part_shape,), (pairs,), [win] * 4 + [near, bias_spec, stat_spec],
        (win,) * 4 + (part_spec,), scratch=scratch(4), estimate=cost(32 * step, 4 << 20),
    )(*ids, ea, oa, eb, ob, qg, bias, final)
    back_eb = chip_swapped(d_eb, 0)
    back_ob = chip_swapped(d_ob, 1)
    back_ea = chip_swapped(joined(d_ea, back_of), 0)
    back_oa = chip_swapped(joined(d_oa, back_ef), 1)
    own_shape = sds((2, rows, half), F32)
    d_a, d_b, dq_own, dq_send = call(
        local_kernel, (own_shape, own_shape, sds((rows, half), BF), sds((rows, half), BF)), (pairs,),
        [win] * 4 + [near, bias_spec, stat_spec, part_spec, far_spec], (win, win, dq_spec, dq_spec),
        scratch=scratch(2), estimate=cost(16 * step, 4 << 20),
    )(*ids, a, b, ef, of, qg, bias, final, dq_near, ds_far)
    dq_got = core_swapped(dq_send)
    q_other, q_own = call(
        query_kernel, (sds((rows, cols), F32), sds((rows, cols), F32)), (1,),
        [whole(rows, half)] * 2 + [whole(2 * cols, cols)], (whole(rows, cols), whole(rows, cols)),
        estimate=cost(2 * rows * cols * 2 * cols, 3 << 20),
    )(*ids, dq_own, dq_got, q_weight)
    d_a, q_other, q_own = lax.optimization_barrier((d_a, q_other, q_own))
    keep, give = call(
        total_kernel, (kv_shape, kv_shape), (1,), [kv_whole] * 6, (kv_whole, kv_whole),
    )(*ids, d_a, d_b, back_ea, back_oa, back_eb, back_ob)
    gave = core_swapped(give)
    weight_keep = pl.BlockSpec((cols, half), lambda i, *p: (1 - p[2][0], p[0][0]))
    weight_gave = pl.BlockSpec((cols, half), lambda i, *p: (1 - p[2][0], 1 - p[0][0]))
    weight_own = pl.BlockSpec((cols, cols), lambda i, *p: (p[2][0], 0))
    add_cost = cost(2 * rows * cols * 2 * half, 2 << 20)
    partial_keep = call(
        add_kernel, sds((rows, cols), F32), (1,), [whole(rows, cols), kv_whole] + [weight_keep] * 2,
        whole(rows, cols), estimate=add_cost,
    )(*ids, q_other, keep, k_weight, v_weight)
    partial_other = call(
        add_kernel, sds((rows, cols), BF), (1,), [whole(rows, cols), kv_whole] + [weight_gave] * 2,
        whole(rows, cols), estimate=add_cost,
    )(*ids, partial_keep, gave, k_weight, v_weight)
    partial_got = lax.ppermute(partial_other, "head", [(0, 1), (1, 0)])
    partial_own = call(
        both_kernel, sds((rows, cols), F32), (1,),
        [whole(rows, cols)] + [kv_whole] * 2 + [weight_own] * 2, whole(rows, cols),
        estimate=cost(2 * rows * cols * 2 * cols, 2 << 20),
    )(*ids, q_own, keep, gave, k_weight, v_weight)
    outgoing = call(
        scatter_kernel, sds((slots, cols), BF), (1,),
        [whole(rows, cols), whole(rows, cols), whole(slots, rows)], whole(slots, cols), placed=False,
        estimate=cost(2 * slots * rows * cols, 2 << 20),
    )(partial_own, partial_got, place)
    arrived = lax.all_to_all(
        outgoing, "blk", split_axis=0, concat_axis=0, tiled=True, axis_index_groups=[order]
    )
    home = [int(g) for g in np.argsort(np.array(order[::4]) // 4)]
    return call(
        functools.partial(restore_kernel, home=home), sds((slots, cols), BF), (1,), [whole(slots, cols)],
        whole(slots, cols), placed=False,
    )(arrived)


def solution(mesh):
    return jax.shard_map(
        on_device,
        mesh=mesh,
        in_specs=(
            P("blk", "head"),
            P("blk", "head"),
            P("blk", "head"),
            P("blk", "head"),
            P(None, "head"),
            P(None, "head"),
            P(None, "head"),
            P("blk", None),
            P("blk", None),
        ),
        out_specs=P("blk", "head"),
        check_vma=False,
    )
```

```python
import functools
import math

import jax
import jax.numpy as jnp
import numpy as np
from jax import lax
from jax.experimental import pallas as pl
from jax.experimental.pallas import tpu as pltpu
from jax.sharding import PartitionSpec as P

HD = 64
BLOCK = 128
REACH = 3
SPAN = 2 * REACH + 1
LOG2E = math.log2(math.e)
MASKED = -1e30
FLOOR = -1e29
CAP = 4
BF = jnp.bfloat16
F32 = jnp.float32
NT = (((1,), (1,)), ((), ()))
NN = (((1,), (0,)), ((), ()))
TN = (((0,), (0,)), ((), ()))


def dot(a, b, dims):
    return lax.dot_general(a, b, dims, preferred_element_type=F32)


def core_swapped(value):
    count = lax.axis_size("blk")
    return lax.ppermute(value, "blk", [(s, s ^ 1) for s in range(count)])


def chip_swapped(value, odd):
    count = lax.axis_size("blk")
    ahead = [-2 if (s // 2) % 2 == odd else 2 for s in range(count)]
    return lax.ppermute(value, "blk", [(s, (s + ahead[s]) % count) for s in range(count)])


def bias_rows(adj_ref):
    shape = (16, 2 * BLOCK)
    row = lax.broadcasted_iota(jnp.int32, shape, 0)
    query_block = lax.broadcasted_iota(jnp.int32, shape, 1) // BLOCK
    allowed = row == 2 * REACH + query_block
    for c in range(2 * SPAN):
        for b in range(2):
            hit = (row == c) & (query_block == b) & (adj_ref[b, c] > 0)
            allowed = allowed | hit
    return jnp.where(allowed, 0.0, MASKED)


def with_place(kernel, core_ref, chip_ref, head_ref, *refs):
    kernel((core_ref[0], chip_ref[0], head_ref[0]), *refs)


def pack_kernel(ids, adj_in_ref, k_ref, v_ref, q_ref, g_ref, send_kv_ref, own_kv_ref, send_qg_ref, own_qg_ref, adj_ref, sems):
    rows, cols = k_ref.shape
    half = cols // 2
    copies = []
    for kv_ref, qg_ref, which in ((send_kv_ref, send_qg_ref, 1 - ids[0]), (own_kv_ref, own_qg_ref, ids[0])):
        at = pl.ds(pl.multiple_of(which * half, half), half)
        for n, from_ref in enumerate((k_ref, v_ref)):
            copies.append(pltpu.make_async_copy(from_ref.at[:, at], kv_ref.at[n], sems.at[len(copies)]))
        for n, from_ref in enumerate((q_ref, g_ref)):
            to = qg_ref.at[0:rows, n * half : (n + 1) * half]
            copies.append(pltpu.make_async_copy(from_ref.at[:, at], to, sems.at[len(copies)]))
    adjacency = pltpu.make_async_copy(adj_in_ref, adj_ref, sems.at[len(copies)])
    adjacency.start()
    for copy in copies:
        copy.start()
    adjacency.wait()
    bias = bias_rows(adj_ref).astype(BF)
    for to_ref in (send_qg_ref, own_qg_ref):
        to_ref[rows : rows + 16, 0:half] = bias
        to_ref[rows : rows + 16, half:] = jnp.zeros((16, half), BF)
    for copy in copies:
        copy.wait()


def order_keys_kernel(ids, own_ref, got_ref, a_ref, b_ref):
    b_own = ids[0] == ids[1]
    own = own_ref[...]
    got = got_ref[...]
    a_ref[...] = jnp.where(b_own, got, own)
    b_ref[...] = jnp.where(b_own, own, got)


def order_queries_kernel(ids, own_ref, got_ref, qg_ref, bias_ref):
    rows, cols = qg_ref.shape[2:]
    scale = 1.0 / math.sqrt(HD)
    for sector, from_ref in ((ids[0], own_ref), (1 - ids[0], got_ref)):
        qg_ref[0, sector] = from_ref[0:rows, 0:cols] * scale
        qg_ref[1, sector] = from_ref[0:rows, cols : 2 * cols]
        bias_ref[sector] = from_ref[rows : rows + 16, 0:cols].astype(F32)


def one_head(pair_ref, h):
    value = pair_ref[...]
    lane_head = lax.broadcasted_iota(jnp.int32, value.shape, 1) // HD
    return jnp.where(lane_head == h, value, 0.0).astype(BF)


def bias_pair_of(bias_ref, t, j):
    return [bias_ref[t, pl.ds(2 * j + b, 1), :] for b in range(2)]


def fold_stats(stats, key_value, query_head, grad_head, bias_pair):
    scores = dot(key_value[0], query_head, NT)
    grads = dot(key_value[1], grad_head, NT)
    top, total, delta = stats
    for b in range(2):
        at = slice(b * BLOCK, (b + 1) * BLOCK)
        new_top = jnp.maximum(top, jnp.max(scores[at], axis=0, keepdims=True) + bias_pair[b])
        weight = jnp.exp2(scores[at] * LOG2E + (bias_pair[b] - new_top) * LOG2E)
        shrink = jnp.exp2((top - new_top) * LOG2E)
        total = jnp.sum(weight, axis=0, keepdims=True) + total * shrink
        delta = jnp.sum(weight * grads[at], axis=0, keepdims=True) + delta * shrink
        top = new_top
    return (top, total, delta), scores, grads


def fold_windows(names, windows, qg_ref, bias_ref, before_ref, stats_ref):
    rows = qg_ref.shape[2]
    for t in range(2):
        for h in range(2):
            qh = one_head(qg_ref.at[0, t], h)
            gh = one_head(qg_ref.at[1, t], h)
            if before_ref is None:
                zero = jnp.zeros((1, rows), F32)
                stats = (zero + FLOOR, zero, zero)
            else:
                stats = tuple(before_ref[t, h, row : row + 1, :] for row in range(3))
            for w, window in zip(names, windows):
                stats, _, _ = fold_stats(stats, window, qh, gh, bias_pair_of(bias_ref, t, w - t))
            for row in range(3):
                stats_ref[t, h, row : row + 1, :] = stats[row]


def first_stats_kernel(ids, a_ref, b_ref, oa_ref, ob_ref, qg_ref, bias_ref, stats_ref):
    odd = ids[1]
    names = (4 - odd, 3 + odd, 2 + 3 * odd, 1 + 5 * odd)
    fold_windows(names, (a_ref, b_ref, oa_ref, ob_ref), qg_ref, bias_ref, None, stats_ref)


def second_stats_kernel(ids, ea_ref, eb_ref, qg_ref, bias_ref, before_ref, stats_ref):
    odd = ids[1]
    names = (5 - 3 * odd, 6 - 5 * odd)
    fold_windows(names, (ea_ref, eb_ref), qg_ref, bias_ref, before_ref, stats_ref)


def head_rows_of(first, second):
    row_head = lax.broadcasted_iota(jnp.int32, first.shape, 0) // HD
    return jnp.where(row_head == 0, first, second)


def query_grad(keys_t, grads, rows):
    both = dot(keys_t, grads, NN)
    return head_rows_of(both[:, 0:rows], both[:, rows:])


def flipped(value):
    return jnp.transpose(value.astype(F32)).astype(BF)


def far_kernel(
    ids, e_ref, o_ref, qg_ref, bias_ref, stats_ref, final_ref, de_ref, do_ref, ds_ref, ps_ref, qs_ref, gs_ref
):
    rows = qg_ref.shape[2]
    odd = ids[1]
    sides = ((1 - odd, e_ref, de_ref), (odd, o_ref, do_ref))
    halves = [slice(b * BLOCK, (b + 1) * BLOCK) for b in range(2)]
    pairs = qg_ref.shape[3] // (2 * HD)
    lanes = [slice(2 * HD * i, 2 * HD * (i + 1)) for i in range(pairs)]
    items = [(i, n, h) for i in range(pairs) for n in range(2) for h in range(2)]
    scores, grads, biases = [], [], []
    for i, n, h in items:
        t, window, _ = sides[n]
        cols = slice(h * rows, (h + 1) * rows)
        qh = one_head(qg_ref.at[0, t, :, lanes[i]], h)
        gh = one_head(qg_ref.at[1, t, :, lanes[i]], h)
        qs_ref[i, n, cols, :] = qh
        gs_ref[i, n, cols, :] = gh
        scores.append(dot(window[0, :, lanes[i]], qh, NT))
        grads.append(dot(window[1, :, lanes[i]], gh, NT))
        biases.append(bias_pair_of(bias_ref, t, (SPAN - 1) * t))
    before = [[stats_ref[sides[n][0], 2 * i + h, row : row + 1, :] for row in range(3)] for i, n, h in items]
    tops = []
    for value, bias, (top, _, _) in zip(scores, biases, before):
        for at, block_bias in zip(halves, bias):
            top = jnp.maximum(top, jnp.max(value[at], axis=0, keepdims=True) + block_bias)
        tops.append(top)
    weights, totals, deltas = [], [], []
    for value, grad, bias, top, (old, total, delta) in zip(scores, grads, biases, tops, before):
        shrink = jnp.exp2((old - top) * LOG2E)
        total = total * shrink
        delta = delta * shrink
        parts = []
        for at, block_bias in zip(halves, bias):
            weight = jnp.exp2(value[at] * LOG2E + (block_bias - top) * LOG2E)
            total = total + jnp.sum(weight, axis=0, keepdims=True)
            delta = delta + jnp.sum(weight * grad[at], axis=0, keepdims=True)
            parts.append(weight)
        weights.append(parts)
        totals.append(total)
        deltas.append(delta)
    for (i, n, h), parts, grad, top, total, delta in zip(items, weights, grads, tops, totals, deltas):
        cols = slice(h * rows, (h + 1) * rows)
        scale = 1.0 / total
        delta = delta * scale
        final_ref[sides[n][0], 2 * i + h, 0:1, :] = top * LOG2E + jnp.log2(total)
        final_ref[sides[n][0], 2 * i + h, 1:2, :] = delta
        for at, weight in zip(halves, parts):
            prob = weight * scale
            ps_ref[i, n, at, cols] = prob.astype(BF)
            ds_ref[i, n, at, cols] = (prob * (grad[at] - delta)).astype(BF)
    for i in range(pairs):
        for n in range(2):
            out_ref = sides[n][2]
            out_ref[0, :, lanes[i]] = dot(ds_ref[i, n], qs_ref[i, n], NN).astype(BF)
            out_ref[1, :, lanes[i]] = dot(ps_ref[i, n], gs_ref[i, n], NN).astype(BF)


def shared_kernel(names, qg_ref, bias_ref, final_ref, windows, outs, ps_ref, ds_ref, qs_ref, gs_ref, kt_ref):
    rows = qg_ref.shape[2]
    for t in range(2):
        for h in range(2):
            block = 2 * t + h
            cols = slice(block * rows, (block + 1) * rows)
            qs_ref[cols, :] = one_head(qg_ref.at[0, t], h)
            gs_ref[cols, :] = one_head(qg_ref.at[1, t], h)
    for n, (w, window) in enumerate(zip(names, windows)):
        keys = slice(n * rows, (n + 1) * rows)
        kt_ref[:, keys] = flipped(window[0])
        for t in range(2):
            for h in range(2):
                block = 2 * t + h
                cols = slice(block * rows, (block + 1) * rows)
                scores = dot(window[0], qs_ref[cols, :], NT)
                grads = dot(window[1], gs_ref[cols, :], NT)
                log_total = final_ref[t, h, 0:1, :]
                delta = final_ref[t, h, 1:2, :]
                bias_pair = bias_pair_of(bias_ref, t, w - t)
                for b in range(2):
                    at = slice(b * BLOCK, (b + 1) * BLOCK)
                    to = slice(n * rows + b * BLOCK, n * rows + (b + 1) * BLOCK)
                    prob = jnp.exp2(scores[at] * LOG2E + (bias_pair[b] * LOG2E - log_total))
                    ps_ref[to, cols] = prob.astype(BF)
                    ds_ref[to, cols] = (prob * (grads[at] - delta)).astype(BF)
        out_ref = outs[n]
        out_ref[0] = dot(ds_ref[keys, :], qs_ref[...], NN).astype(out_ref.dtype)
        out_ref[1] = dot(ps_ref[keys, :], gs_ref[...], NN).astype(out_ref.dtype)
    return [
        query_grad(kt_ref[...], ds_ref[:, 2 * t * rows : 2 * (t + 1) * rows], rows) for t in range(2)
    ]


def near_kernel(ids, ea_ref, oa_ref, eb_ref, ob_ref, qg_ref, bias_ref, final_ref, *refs):
    outs, dq_ref, scratch = refs[0:4], refs[4], refs[5:]
    odd = ids[1]
    names = (5 - 3 * odd, 2 + 3 * odd, 6 - 5 * odd, 1 + 5 * odd)
    grads = shared_kernel(names, qg_ref, bias_ref, final_ref, (ea_ref, oa_ref, eb_ref, ob_ref), outs, *scratch)
    for t in range(2):
        dq_ref[0, t] = grads[t]


def local_kernel(ids, a_ref, b_ref, ef_ref, of_ref, qg_ref, bias_ref, final_ref, part_ref, far_ref, *refs):
    outs, (dq_own_ref, dq_send_ref), scratch = refs[0:2], refs[2:4], refs[4:]
    rows = qg_ref.shape[2]
    odd = ids[1]
    grads = shared_kernel((4 - odd, 3 + odd), qg_ref, bias_ref, final_ref, (a_ref, b_ref), outs, *scratch)
    far_e = query_grad(flipped(ef_ref[0]), far_ref[0, 0], rows)
    far_o = query_grad(flipped(of_ref[0]), far_ref[0, 1], rows)
    even = odd == 0
    far = (jnp.where(even, far_o, far_e), jnp.where(even, far_e, far_o))
    total = [part_ref[0, t] + grads[t] + far[t] for t in range(2)]
    first = ids[0] == 0
    scale = 1.0 / math.sqrt(HD)
    dq_own_ref[...] = jnp.transpose(jnp.where(first, total[0], total[1]) * scale).astype(BF)
    dq_send_ref[...] = jnp.transpose(jnp.where(first, total[1], total[0]) * scale).astype(BF)


def joined(first, second):
    return (first.astype(F32) + second.astype(F32)).astype(BF)


def total_kernel(ids, a_ref, b_ref, ea_ref, oa_ref, eb_ref, ob_ref, keep_ref, send_ref):
    b_own = ids[0] == ids[1]
    for which in range(2):
        value_a = a_ref[which] + ob_ref[which].astype(F32) + ea_ref[which].astype(F32)
        value_b = b_ref[which] + eb_ref[which].astype(F32) + oa_ref[which].astype(F32)
        keep_ref[which] = jnp.where(b_own, value_b, value_a).astype(BF)
        send_ref[which] = jnp.where(b_own, value_a, value_b).astype(BF)


def query_kernel(ids, own_ref, got_ref, weight_ref, other_out_ref, own_out_ref):
    first = ids[0] == 0
    half = own_ref.shape[1]
    low = jnp.where(first, own_ref[...], got_ref[...])
    high = jnp.where(first, got_ref[...], own_ref[...])
    cols = own_out_ref.shape[1]
    here = ids[2]
    for out_ref, which in ((other_out_ref, 1 - here), (own_out_ref, here)):
        at = pl.ds(pl.multiple_of(which * cols, cols), cols)
        out_ref[...] = dot(low, weight_ref[at, 0:half], NT) + dot(high, weight_ref[at, half:], NT)


def add_kernel(ids, base_ref, grads_ref, wk_ref, wv_ref, out_ref):
    value = base_ref[...] + dot(grads_ref[0], wk_ref[...], NT) + dot(grads_ref[1], wv_ref[...], NT)
    out_ref[...] = value.astype(out_ref.dtype)


def both_kernel(ids, base_ref, keep_ref, gave_ref, wk_ref, wv_ref, out_ref):
    first = ids[0] == 0
    half = keep_ref.shape[2]
    value = base_ref[...]
    for which, weight in ((0, wk_ref), (1, wv_ref)):
        low = jnp.where(first, keep_ref[which], gave_ref[which])
        high = jnp.where(first, gave_ref[which], keep_ref[which])
        value = value + dot(low, weight[:, 0:half], NT) + dot(high, weight[:, half:], NT)
    out_ref[...] = value


def route_kernel(owner_col_ref, owner_row_ref, label_ref, place_ref):
    rows = owner_col_ref.shape[0]
    owner_row = owner_row_ref[...]
    earlier = lax.broadcasted_iota(jnp.int32, (rows, rows), 0) < lax.broadcasted_iota(jnp.int32, (rows, rows), 1)
    same = (owner_col_ref[...] == owner_row) & earlier
    rank = jnp.sum(same.astype(jnp.int32), axis=0, keepdims=True)
    target = owner_row * CAP + rank
    place_ref[...] = jnp.where(label_ref[...] == target, 1.0, 0.0).astype(BF)


def scatter_kernel(own_ref, got_ref, place_ref, out_ref):
    value = (own_ref[...] + got_ref[...].astype(F32)).astype(BF)
    out_ref[...] = dot(place_ref[...], value, NN).astype(BF)


def spread_order(count):
    groups = [int(g) for g in np.random.default_rng(8).permutation(count // 4)]
    return [4 * g + i for g in groups for i in range(4)]


def restore_kernel(from_ref, out_ref, *, home):
    rows = out_ref.shape[0] // len(home)
    for i, g in enumerate(home):
        out_ref[i * rows : (i + 1) * rows, :] = from_ref[g * rows : (g + 1) * rows, :]


def cost(flops, moved_bytes, exps=0):
    return pl.CostEstimate(flops=flops, bytes_accessed=moved_bytes, transcendentals=exps)


def on_device(query, key, value, out_grad, q_weight, k_weight, v_weight, adjacency, owner):
    rows, cols = query.shape
    half = cols // 2
    pair = 2 * HD
    sds = jax.ShapeDtypeStruct
    block = lax.axis_index("blk")
    ids = tuple(
        jnp.reshape(value, (1,)).astype(jnp.int32)
        for value in (block & 1, 1 - ((block >> 1) & 1), lax.axis_index("head"))
    )
    smem = pl.BlockSpec(memory_space=pltpu.SMEM)
    hbm = pl.BlockSpec(memory_space=pltpu.HBM)

    def call(kernel, outs, grid, in_specs, out_specs, scratch=(), placed=True, estimate=None, limit=16):
        return pl.pallas_call(
            functools.partial(with_place, kernel) if placed else kernel,
            out_shape=outs,
            grid_spec=pltpu.PrefetchScalarGridSpec(
                num_scalar_prefetch=3 if placed else 0, grid=grid, in_specs=in_specs, out_specs=out_specs,
                scratch_shapes=list(scratch),
            ),
            compiler_params=pltpu.CompilerParams(vmem_limit_bytes=limit << 20),
            cost_estimate=estimate,
        )

    def whole(*shape):
        return pl.BlockSpec(shape, lambda i, *p: (0,) * len(shape))

    kv_shape = sds((2, rows, half), BF)
    kv_whole = whole(2, rows, half)
    qg_packed = sds((rows + 16, 2 * half), BF)
    packed_whole = whole(rows + 16, 2 * half)
    send_kv, own_kv, send_qg, own_qg = call(
        pack_kernel, (kv_shape, kv_shape, qg_packed, qg_packed), (1,), [hbm] * 5,
        (kv_whole, kv_whole, packed_whole, packed_whole),
        scratch=(pltpu.SMEM(adjacency.shape, jnp.int32), pltpu.SemaphoreType.DMA((9,))),
    )(*ids, *[pltpu.with_memory_space_constraint(x, pltpu.HBM) for x in (adjacency, key, value, query, out_grad)])
    got_kv = core_swapped(send_kv)
    a, b = call(order_keys_kernel, (kv_shape, kv_shape), (1,), [kv_whole] * 2, (kv_whole, kv_whole))(
        *ids, own_kv, got_kv
    )
    send_qg, a, b = lax.optimization_barrier((send_qg, a, b))
    got_qg = core_swapped(send_qg)
    qg, bias = call(
        order_queries_kernel, (sds((2, 2, rows, half), BF), sds((2, 16, rows), F32)), (1,),
        [packed_whole] * 2, (whole(2, 2, rows, half), whole(2, 16, rows)),
    )(*ids, own_qg, got_qg)
    ea = chip_swapped(a, 0)
    oa = chip_swapped(b, 1)
    eb = chip_swapped(b, 0)
    ob = chip_swapped(a, 1)
    ef = chip_swapped(oa, 0)
    of = chip_swapped(ea, 1)

    count = lax.axis_size("blk")
    slots = CAP * count
    order = spread_order(count)
    labels = jnp.asarray(np.array([[CAP * s + r] for s in order for r in range(CAP)], np.int32))
    place = call(
        route_kernel, sds((slots, rows), BF), (1,),
        [whole(rows, 1), whole(1, rows), whole(slots, 1)], whole(slots, rows), placed=False,
        estimate=cost(rows * rows * 8, 1 << 20),
    )(owner, owner.reshape(1, rows), labels)

    pairs = half // pair
    win = pl.BlockSpec((2, rows, pair), lambda i, *p: (0, 0, i))
    near = pl.BlockSpec((2, 2, rows, pair), lambda i, *p: (0, 0, 0, i))
    dq_spec = pl.BlockSpec((rows, pair), lambda i, *p: (0, i))
    stat_spec = pl.BlockSpec((2, 2, 8, rows), lambda i, *p: (0, i, 0, 0))
    bias_spec = whole(2, 16, rows)
    stat_shape = sds((2, 2 * pairs, 8, rows), F32)
    step = 2 * rows * rows * HD * 4
    part_shape = sds((pairs, 2, pair, rows), F32)
    part_spec = pl.BlockSpec((1, 2, pair, rows), lambda i, *p: (i, 0, 0, 0))

    def scratch(blocks):
        return (
            pltpu.VMEM((blocks * rows, 4 * rows), BF),
            pltpu.VMEM((blocks * rows, 4 * rows), BF),
            pltpu.VMEM((4 * rows, pair), BF),
            pltpu.VMEM((4 * rows, pair), BF),
            pltpu.VMEM((pair, blocks * rows), BF),
        )

    stats = call(
        first_stats_kernel, stat_shape, (pairs,), [win] * 4 + [near, bias_spec], stat_spec,
        estimate=cost(16 * step, 4 << 20),
    )(*ids, a, b, oa, ob, qg, bias)
    stats = call(
        second_stats_kernel, stat_shape, (pairs,), [win] * 2 + [near, bias_spec, stat_spec], stat_spec,
        estimate=cost(8 * step, 2 << 20),
    )(*ids, ea, eb, qg, bias, stats)
    stats, place = lax.optimization_barrier((stats, place))
    far_rows = pltpu.VMEM((pairs, 2, 2 * rows, pair), BF)
    far_shape = sds((pairs, 2, rows, 2 * rows), BF)
    far_spec = pl.BlockSpec((1, 2, rows, 2 * rows), lambda i, *p: (i, 0, 0, 0))
    stat_whole = whole(2, 2 * pairs, 8, rows)
    final, d_ef, d_of, ds_far = call(
        far_kernel, (stat_shape, kv_shape, kv_shape, far_shape), (1,),
        [kv_whole] * 2 + [whole(2, 2, rows, half), bias_spec, stat_whole],
        (stat_whole, kv_whole, kv_whole, whole(pairs, 2, rows, 2 * rows)),
        scratch=(pltpu.VMEM((pairs, 2, rows, 2 * rows), BF), far_rows, far_rows), estimate=cost(8 * step, 2 << 20),
    )(*ids, ef, of, qg, bias, stats)
    back_ef = chip_swapped(d_ef, 0)
    back_of = chip_swapped(d_of, 1)
    d_ea, d_oa, d_eb, d_ob, dq_near = call(
        near_kernel, (kv_shape,) * 4 + (part_shape,), (pairs,), [win] * 4 + [near, bias_spec, stat_spec],
        (win,) * 4 + (part_spec,), scratch=scratch(4), estimate=cost(32 * step, 4 << 20),
    )(*ids, ea, oa, eb, ob, qg, bias, final)
    back_eb = chip_swapped(d_eb, 0)
    back_ob = chip_swapped(d_ob, 1)
    back_ea = chip_swapped(joined(d_ea, back_of), 0)
    back_oa = chip_swapped(joined(d_oa, back_ef), 1)
    own_shape = sds((2, rows, half), F32)
    d_a, d_b, dq_own, dq_send = call(
        local_kernel, (own_shape, own_shape, sds((rows, half), BF), sds((rows, half), BF)), (pairs,),
        [win] * 4 + [near, bias_spec, stat_spec, part_spec, far_spec], (win, win, dq_spec, dq_spec),
        scratch=scratch(2), estimate=cost(16 * step, 4 << 20),
    )(*ids, a, b, ef, of, qg, bias, final, dq_near, ds_far)
    dq_got = core_swapped(dq_send)
    q_other, q_own = call(
        query_kernel, (sds((rows, cols), F32), sds((rows, cols), F32)), (1,),
        [whole(rows, half)] * 2 + [whole(2 * cols, cols)], (whole(rows, cols), whole(rows, cols)),
        estimate=cost(2 * rows * cols * 2 * cols, 3 << 20),
    )(*ids, dq_own, dq_got, q_weight)
    d_a, q_other, q_own = lax.optimization_barrier((d_a, q_other, q_own))
    keep, give = call(
        total_kernel, (kv_shape, kv_shape), (1,), [kv_whole] * 6, (kv_whole, kv_whole),
    )(*ids, d_a, d_b, back_ea, back_oa, back_eb, back_ob)
    gave = core_swapped(give)
    weight_keep = pl.BlockSpec((cols, half), lambda i, *p: (1 - p[2][0], p[0][0]))
    weight_gave = pl.BlockSpec((cols, half), lambda i, *p: (1 - p[2][0], 1 - p[0][0]))
    weight_own = pl.BlockSpec((cols, cols), lambda i, *p: (p[2][0], 0))
    add_cost = cost(2 * rows * cols * 2 * half, 2 << 20)
    partial_keep = call(
        add_kernel, sds((rows, cols), F32), (1,), [whole(rows, cols), kv_whole] + [weight_keep] * 2,
        whole(rows, cols), estimate=add_cost,
    )(*ids, q_other, keep, k_weight, v_weight)
    partial_other = call(
        add_kernel, sds((rows, cols), BF), (1,), [whole(rows, cols), kv_whole] + [weight_gave] * 2,
        whole(rows, cols), estimate=add_cost,
    )(*ids, partial_keep, gave, k_weight, v_weight)
    partial_got = lax.ppermute(partial_other, "head", [(0, 1), (1, 0)])
    partial_own = call(
        both_kernel, sds((rows, cols), F32), (1,),
        [whole(rows, cols)] + [kv_whole] * 2 + [weight_own] * 2, whole(rows, cols),
        estimate=cost(2 * rows * cols * 2 * cols, 2 << 20),
    )(*ids, q_own, keep, gave, k_weight, v_weight)
    outgoing = call(
        scatter_kernel, sds((slots, cols), BF), (1,),
        [whole(rows, cols), whole(rows, cols), whole(slots, rows)], whole(slots, cols), placed=False,
        estimate=cost(2 * slots * rows * cols, 2 << 20),
    )(partial_own, partial_got, place)
    arrived = lax.all_to_all(
        outgoing, "blk", split_axis=0, concat_axis=0, tiled=True, axis_index_groups=[order]
    )
    home = [int(g) for g in np.argsort(np.array(order[::4]) // 4)]
    return call(
        functools.partial(restore_kernel, home=home), sds((slots, cols), BF), (1,), [whole(slots, cols)],
        whole(slots, cols), placed=False,
    )(arrived)


def solution(mesh):
    return jax.shard_map(
        on_device,
        mesh=mesh,
        in_specs=(
            P("blk", "head"),
            P("blk", "head"),
            P("blk", "head"),
            P("blk", "head"),
            P(None, "head"),
            P(None, "head"),
            P(None, "head"),
            P("blk", None),
            P("blk", None),
        ),
        out_specs=P("blk", "head"),
        check_vma=False,
    )
```
